512 devices in a mesh: dp: 32 (over y, z_hi), seq: 16 (over x, z_lo, core).
Axes of the slice: x: 4, y: 8, z: 8 (z_hi: 4, z_lo: 2; z = z_hi * 2 + z_lo), core: 2. Of those that a mesh axis runs over, the one named last changes fastest.
Arguments:
- queries: bfloat16 [32, 2048, 2048], P('dp', 'seq'), may hold values from -6 to 6
- grad_out: bfloat16 [32, 2048, 2048], P('dp', 'seq'), may hold values from -6 to 6
- encoded: bfloat16 [32, 32, 64, 896], P('dp', 'seq'), may hold values from -6 to 6
- kv_weight: bfloat16 [896, 4096], P(None, 'dp'), may hold values from -0.1875 to 0.1875
- neighbour_ids: int32 [32, 32, 2], P('dp', 'seq'), may hold values from 0 to 31, all different within a row
- slot_map: int32 [32, 32], P('dp'), may hold values from 0 to 31, each once within a row
Outputs:
- attended: bfloat16 [32, 2048, 2048], P('dp', 'seq')
- grad_queries: bfloat16 [32, 2048, 2048], P('dp', 'seq')
- grad_encoded: float32 [32, 32, 64, 896], P('dp', 'seq')
The draws below stay inside these ranges and needn't reach their ends.
Inputs may be any that keep to these rules, and one draw needn't show every extreme that they name: `neighbour_ids`: each span names 2 different neighbour ids of its own sequence. `slot_map`: for each sequence a permutation; storage position p lies on the seq index p // 2.
All inputs are finite; a program needn't handle non-finite values.
Results may differ from the reference program's by a relative error of at most 0.018.
Values may be sent and summed in bfloat16 or wider, within the bound.
A program may use at most 64 MiB of HBM per device.

```python
import jax
import jax.numpy as jnp
from jax import lax

DE = 896
HEAD_SIZE = 128
HEADS = 16
SPAN = 64
NLEN = 64
READS = 2
HD = 2048
SPAN_DEV = 2
LENGTH = 2048
SPANS = 32
NBR_GROUP = 32
SEQS = 32
N_SEQ = 16


def level_of(key, dims, split, least, largest):
    gain = 1.0
    for axis_at, blocks in split:
        draws = jax.random.uniform(jax.random.fold_in(jax.random.fold_in(key, 6), axis_at), (blocks,), jnp.float32, least / len(split), largest / len(split))
        gain = gain * jnp.repeat(jnp.exp(draws), dims[axis_at] // blocks).reshape((-1,) + (1,) * (len(dims) - 1 - axis_at))
    return gain


def different_ones(stream_key, rows, count, top, lift):
    sequence = jax.random.permutation(jax.random.fold_in(stream_key, 1), count)
    boost = sequence
    for power in range(3):
        boost = boost * boost // count
    boost = boost * lift // count
    tickets = jax.random.randint(jax.random.fold_in(stream_key, 2), (rows, count), 0, 4096) + boost
    sure = jax.random.permutation(jax.random.fold_in(stream_key, 3), rows)[jnp.arange(count) % rows]
    tickets = jnp.where(jnp.arange(rows)[:, None] == sure[None, :], 1 << 14, tickets)
    score = tickets * count + jnp.arange(count)
    return lax.top_k(score.astype(jnp.int32), top)[1].astype(jnp.int32)


def noise(stream_key, dims, scale, bound, cuts=(), held_as=jnp.bfloat16):
    result = jax.random.normal(stream_key, dims, jnp.float32) * scale
    if len(cuts) > 0:
        result = level_of(stream_key, dims, cuts, -0.22, 0.18) * result
    return jnp.clip(result, min=-bound, max=bound).astype(held_as)


def setup_inputs(seed: int = 0) -> dict:
    key_of = jax.random.split(jax.random.key(seed), 7)
    return {
        "queries": noise(key_of[0], (SEQS, LENGTH, HD), 1.0, 6.0, ((0, 32), (1, 16))),
        "grad_out": noise(key_of[1], (SEQS, LENGTH, HD), 1.0, 6.0, ((0, 32), (1, 16))),
        "encoded": noise(key_of[2], (SEQS, NBR_GROUP, NLEN, DE), 1.0, 6.0, ((0, 32), (1, 16))),
        "kv_weight": noise(key_of[3], (DE, 2 * HD), DE ** -0.5, 0.1875, ((1, 32),)),
        "neighbour_ids": different_ones(key_of[4], SEQS * SPANS, NBR_GROUP, READS, 1024).reshape((SEQS, SPANS, READS)),
        "slot_map": jax.vmap(lambda own: jax.random.permutation(own, NBR_GROUP))(jax.random.split(key_of[5], SEQS)).reshape((SEQS, NBR_GROUP)).astype(jnp.int32),
    }


def one_sequence(kv_weight, packed):
    query_rows, grad_rows, stored, chosen, slots = packed
    hidden = HEADS * HEAD_SIZE
    scale_factor = HEAD_SIZE ** -0.5
    projected = jnp.dot(stored.reshape(NBR_GROUP * NLEN, DE), kv_weight, preferred_element_type=jnp.float32)
    kv_rows = projected.astype(jnp.bfloat16).reshape(NBR_GROUP, NLEN, 2 * hidden)
    matches = chosen[:, :, None] == jnp.arange(NBR_GROUP, dtype=jnp.int32)[None, None, :]
    positions = jnp.sum(jnp.where(matches, slots[None, None, :], 0), axis=2).astype(jnp.int32)
    flat_pos = positions.reshape(SPANS * READS)
    kv_reads = jnp.take(kv_rows, flat_pos, axis=0).reshape(SPANS, READS * NLEN, 2 * hidden)
    keys = kv_reads[:, :, :hidden].reshape(SPANS, READS * NLEN, HEADS, HEAD_SIZE).astype(jnp.float32)
    values = kv_reads[:, :, hidden:].reshape(SPANS, READS * NLEN, HEADS, HEAD_SIZE).astype(jnp.float32)
    query_tiles = query_rows.reshape(SPANS, SPAN, HEADS, HEAD_SIZE).astype(jnp.float32)
    grad_tiles = grad_rows.reshape(SPANS, SPAN, HEADS, HEAD_SIZE).astype(jnp.float32)
    scores = jnp.einsum('cqhd,ckhd->chqk', query_tiles, keys) * scale_factor
    expos = jnp.exp(scores)
    probs = expos / jnp.sum(expos, axis=-1, keepdims=True)
    probs_low = probs.astype(jnp.bfloat16).astype(jnp.float32)
    attended = jnp.einsum('chqk,ckhd->cqhd', probs_low, values).astype(jnp.bfloat16).reshape(LENGTH, hidden)
    d_probs = jnp.einsum('cqhd,ckhd->chqk', grad_tiles, values)
    delta = jnp.sum(probs * d_probs, axis=-1, keepdims=True)
    d_scores = (probs * (d_probs - delta) * scale_factor).astype(jnp.bfloat16).astype(jnp.float32)
    grad_queries = jnp.einsum('chqk,ckhd->cqhd', d_scores, keys).astype(jnp.bfloat16).reshape(LENGTH, hidden)
    d_keys = jnp.einsum('chqk,cqhd->ckhd', d_scores, query_tiles).reshape(SPANS * READS, NLEN, hidden)
    d_values = jnp.einsum('chqk,cqhd->ckhd', probs_low, grad_tiles).reshape(SPANS * READS, NLEN, hidden)
    grad_reads = jnp.concatenate([d_keys, d_values], axis=-1).astype(jnp.bfloat16)
    enc_reads = jnp.dot(grad_reads.reshape(SPANS * READS * NLEN, 2 * hidden), kv_weight.T, preferred_element_type=jnp.float32)
    grad_blocks = enc_reads.reshape(N_SEQ, SPAN_DEV * READS, NLEN, DE)
    pos_blocks = flat_pos.reshape(N_SEQ, SPAN_DEV * READS)
    onehot = (pos_blocks[:, :, None] == jnp.arange(NBR_GROUP, dtype=jnp.int32)[None, None, :]).astype(jnp.float32)
    partial_value = jnp.einsum('brn,brlk->bnlk', onehot, grad_blocks, precision=lax.Precision.HIGHEST)
    rounded = lax.optimization_barrier(partial_value.astype(jnp.bfloat16))
    grad_encoded = jnp.sum(rounded.astype(jnp.float32), axis=0)
    return attended, grad_queries, grad_encoded


def reference(queries, grad_out, encoded, kv_weight, neighbour_ids, slot_map):
    return lax.map(lambda packed: one_sequence(kv_weight, packed), (queries, grad_out, encoded, neighbour_ids, slot_map))
```

```python
import jax
import jax.numpy as jnp
from jax import lax
from jax.experimental import pallas as pl
from jax.experimental.pallas import tpu as pltpu
from jax.sharding import PartitionSpec as P

MESH = pl.DeviceIdType.MESH
BF = jnp.bfloat16
F32 = jnp.float32

HS = 128
HEADS = 16
SPAN = 64
NLEN = 64
DE = 896
NSH = 32
NSEQ = 16
HALF = DE // 2
QTR = HALF // 2
SCALE = HS ** -0.5


class Sems:
    def __init__(self):
        self.at = {}

    def __call__(self, *name):
        return self.at.setdefault(name, len(self.at))


def nt(a, b):
    return lax.dot_general(a, b, (((1,), (1,)), ((), ())), preferred_element_type=F32)


def tn(a, b):
    return lax.dot_general(a, b, (((0,), (0,)), ((), ())), preferred_element_type=F32)


def nn(a, b):
    return lax.dot_general(a, b, (((1,), (0,)), ((), ())), preferred_element_type=F32)


NSEM = 176


def kernel(
    q_hbm, g_hbm, enc_hbm, w_hbm, ids_s, slot_s, ids_hbm,
    att_hbm, dq_hbm, ge_hbm,
    wbuf, encbuf, qg, qgw, xrd, pbuf, dsbuf, acc, own16, sib16,
    xsend, xrecv, zsend, zrecv, gout, attv, dqv, px, sibids_v, sibids_s,
    ssem, rsem, lsem,
):
    dp = lax.axis_index("dp")
    sq = lax.axis_index("seq")
    y, k = dp // 4, dp % 4
    x, zl, c = sq // 4, (sq // 2) % 2, sq % 2
    o = 2 * zl - 1
    right_y = (((y + 1) % 8) * 4 + k, sq)
    left_y = (((y + 7) % 8) * 4 + k, sq)
    sq_in = sq + 2 - 4 * zl
    outer = (y * 4 + (k + o + 4) % 4, sq_in)
    inner = (dp, sq_in)
    right_x = (dp, (sq + 4) % NSEQ)
    left_x = (dp, (sq + 12) % NSEQ)
    sib = (dp, sq + 1 - 2 * c)
    sem = Sems()
    sent = {0: [], 1: [], 2: []}

    def send(who, name, src, dst, dev):
        i = sem(*name)
        pltpu.make_async_remote_copy(src, dst, ssem.at[i], rsem.at[i], device_id=dev, device_id_type=MESH).start()
        sent[who].append((i, src, dev))

    def recv(name, dst, dev):
        i = sem(*name)
        pltpu.make_async_remote_copy(dst, dst, ssem.at[i], rsem.at[i], device_id=dev, device_id_type=MESH).wait_recv()

    loads = [
        pltpu.make_async_copy(w_hbm, wbuf.at[dp], lsem.at[0]),
        pltpu.make_async_copy(enc_hbm, encbuf.at[sq], lsem.at[1]),
        pltpu.make_async_copy(q_hbm, qg.at[0], lsem.at[2]),
        pltpu.make_async_copy(g_hbm, qg.at[1], lsem.at[3]),
    ]
    for cp in loads:
        cp.start()
    barrier = pltpu.get_barrier_semaphore()
    for dev in (right_y, left_y, outer, inner, right_x, left_x, sib):
        pl.semaphore_signal(barrier, inc=1, device_id=dev, device_id_type=MESH)
    loads[0].wait()
    loads[1].wait()
    pl.semaphore_wait(barrier, 7)

    def shard(dy, kk):
        return ((y + dy + 8) % 8) * 4 + (kk + 8) % 4

    def seq_of(dx, zz):
        return ((x + dx + 4) % 4) * 4 + zz * 2 + c

    def enc_start():
        mine = encbuf.at[sq]
        send(2, ("ea", "r"), mine, mine, right_x)
        send(2, ("ea", "l"), mine, mine, left_x)
        send(2, ("ez",), mine, mine, inner)
        send(2, ("es", 0), mine, mine, sib)
        send(2, ("ids",), ids_hbm, sibids_v, sib)

    def enc_z():
        ref = encbuf.at[seq_of(0, 1 - zl)]
        recv(("ez",), ref, inner)
        send(2, ("eb", "r"), ref, ref, right_x)
        send(2, ("eb", "l"), ref, ref, left_x)
        send(2, ("es", 1), ref, ref, sib)

    def enc_1():
        ref = encbuf.at[seq_of(-1, zl)]
        recv(("ea", "r"), ref, left_x)
        send(2, ("e2", "r"), ref, ref, right_x)
        send(2, ("es", 2), ref, ref, sib)
        ref = encbuf.at[seq_of(1, zl)]
        recv(("ea", "l"), ref, right_x)
        send(2, ("es", 3), ref, ref, sib)

    def enc_2():
        ref = encbuf.at[seq_of(1, 1 - zl)]
        recv(("eb", "l"), ref, right_x)
        send(2, ("e2", "l"), ref, ref, left_x)
        send(2, ("es", 4), ref, ref, sib)
        ref = encbuf.at[seq_of(-1, 1 - zl)]
        recv(("eb", "r"), ref, left_x)
        send(2, ("es", 5), ref, ref, sib)

    def enc_3():
        ref = encbuf.at[seq_of(2, zl)]
        recv(("e2", "r"), ref, left_x)
        send(2, ("es", 6), ref, ref, sib)
        ref = encbuf.at[seq_of(2, 1 - zl)]
        recv(("e2", "l"), ref, right_x)
        send(2, ("es", 7), ref, ref, sib)

    def enc_sib():
        cs = 1 - c
        for i, (dx, zz) in enumerate(((0, zl), (0, 1 - zl), (-1, zl), (1, zl), (1, 1 - zl), (-1, 1 - zl), (2, zl), (2, 1 - zl))):
            recv(("es", i), encbuf.at[((x + dx + 4) % 4) * 4 + zz * 2 + cs], sib)

    OFFS = (0, -1, 1, -2, 2, -3, 3, 4)

    def wp(d, r0=0, n=HALF, core=0):
        return wbuf.at[d, pl.ds(core * HALF + r0, n)]

    def to_sib(core, dy, kk, tag):
        ref = wp(shard(dy, kk), core=core)
        send(core, ("ws", core, dy, tag), ref, ref, sib)

    def core0(n):
        if n < 8:
            dy = OFFS[n]
            d = shard(dy, k)
            if dy == 0:
                send(0, ("yr", 1), wp(d), wp(d), right_y)
                send(0, ("yl", 1), wp(d), wp(d), left_y)
            elif dy == 4:
                recv(("yr", 4), wp(d, 0, QTR), left_y)
                recv(("yl", 4), wp(d, QTR, QTR), right_y)
            elif dy < 0:
                recv(("yr", -dy), wp(d), left_y)
                part = (0, HALF) if dy > -3 else (0, QTR)
                send(0, ("yr", 1 - dy), wp(d, *part), wp(d, *part), right_y)
            else:
                recv(("yl", dy), wp(d), right_y)
                part = (0, HALF) if dy < 3 else (QTR, QTR)
                send(0, ("yl", 1 + dy), wp(d, *part), wp(d, *part), left_y)
            send(0, ("zo", dy), wp(d), wp(d), outer)
            if dy != 0:
                to_sib(0, dy, k, 0)
        if 1 <= n < 9:
            dy = OFFS[n - 1]
            d = shard(dy, k + o)
            recv(("zo", dy), wp(d), outer)
            send(0, ("zi", dy), wp(d), wp(d), inner)
            to_sib(0, dy, k + o, 1)
        if 2 <= n < 10:
            dy = OFFS[n - 2]
            d = shard(dy, k - o)
            recv(("zi", dy), wp(d), inner)
            part = pl.multiple_of((1 - zl) * QTR, QTR)
            send(0, ("zoh", dy), wp(d, part, QTR), wp(d, part, QTR), outer)
            to_sib(0, dy, k - o, 2)
        if 3 <= n < 11:
            dy = OFFS[n - 3]
            d = shard(dy, k + 2)
            part = pl.multiple_of(zl * QTR, QTR)
            recv(("zoh", dy), wp(d, part, QTR), outer)
            send(0, ("zih", dy), wp(d, part, QTR), wp(d, part, QTR), inner)
        if 4 <= n < 12:
            dy = OFFS[n - 4]
            d = shard(dy, k + 2)
            part = pl.multiple_of((1 - zl) * QTR, QTR)
            recv(("zih", dy), wp(d, part, QTR), inner)
            to_sib(0, dy, k + 2, 3)

    def w1(d, r0=0, n=HALF):
        return wp(d, r0, n, core=1)

    KK = (lambda: k, lambda: k + o, lambda: k - o, lambda: k + 2)

    def c1_y(m):
        d = shard(0, KK[m]())
        send(1, ("cr", 1, m), w1(d), w1(d), right_y)
        send(1, ("cl", 1, m), w1(d), w1(d), left_y)
        if m:
            to_sib(1, 0, KK[m](), m)

    def c1_step(s, m):
        kk = KK[m]()
        if s < 4:
            d = shard(-s, kk)
            recv(("cr", s, m), w1(d), left_y)
            part = (0, HALF) if s < 3 else (0, QTR)
            send(1, ("cr", s + 1, m), w1(d, *part), w1(d, *part), right_y)
            to_sib(1, -s, kk, m)
            d = shard(s, kk)
            recv(("cl", s, m), w1(d), right_y)
            part = (0, HALF) if s < 3 else (QTR, QTR)
            send(1, ("cl", s + 1, m), w1(d, *part), w1(d, *part), left_y)
            to_sib(1, s, kk, m)
        else:
            d = shard(4, kk)
            recv(("cr", 4, m), w1(d, 0, QTR), left_y)
            recv(("cl", 4, m), w1(d, QTR, QTR), right_y)
            to_sib(1, 4, kk, m)

    def core1(n):
        if n == 0:
            d = shard(0, k)
            send(1, ("dzo",), w1(d), w1(d), outer)
            c1_y(0)
        elif n == 1:
            d = shard(0, k + o)
            recv(("dzo",), w1(d), outer)
            send(1, ("dzi",), w1(d), w1(d), inner)
            c1_y(1)
            c1_step(1, 0)
        elif n == 2:
            d = shard(0, k - o)
            recv(("dzi",), w1(d), inner)
            part = pl.multiple_of((1 - zl) * QTR, QTR)
            send(1, ("dzoh",), w1(d, part, QTR), w1(d, part, QTR), outer)
            c1_y(2)
            c1_step(1, 1)
        elif n == 3:
            d = shard(0, k + 2)
            part = pl.multiple_of(zl * QTR, QTR)
            recv(("dzoh",), w1(d, part, QTR), outer)
            send(1, ("dzih",), w1(d, part, QTR), w1(d, part, QTR), inner)
            part = pl.multiple_of((1 - zl) * QTR, QTR)
            recv(("dzih",), w1(d, part, QTR), inner)
            c1_y(3)
            c1_step(1, 2)
        else:
            for s, m in {4: ((1, 3), (2, 0)), 5: ((2, 1), (2, 2)), 6: ((2, 3), (3, 0)), 7: ((3, 1), (3, 2)),
                         8: ((3, 3), (4, 0)), 9: ((4, 1), (4, 2)), 10: ((4, 3),), 11: ()}[n]:
                c1_step(s, m)

    def stage(n):
        @pl.when(c == 0)
        def _():
            core0(n)

        @pl.when(c == 1)
        def _():
            core1(n)

    def from_sib(dys):
        @pl.when(c == 0)
        def _():
            for dy in dys:
                for m in range(4):
                    if dy or m:
                        recv(("ws", 1, dy, m), w1(shard(dy, KK[m]())), sib)

        @pl.when(c == 1)
        def _():
            for dy in dys:
                for m in range(4):
                    if dy or m:
                        recv(("ws", 0, dy, m), wp(shard(dy, KK[m]())), sib)

    def project(dy):
        base = ((y + dy + 8) % 8) * 4

        def one(i, _):
            d = base + i
            t = d // HEADS
            h = d % HEADS
            lhs = qg[t, :, pl.ds(pl.multiple_of(h * HS, HS), HS)]
            qgw[d] = nt(lhs, wbuf[d]).astype(BF)
            return 0

        lax.fori_loop(0, 4, one, 0)

    def attend(dy, first):
        g = (y + dy + 8) % 4

        def one(s, _):
            rows = pl.ds(pl.multiple_of(s * SPAN, SPAN), SPAN)
            xs = xrd[s]
            qw = qgw[pl.ds(g * 4, 4), rows, :].reshape(4 * SPAN, DE)
            gw = qgw[pl.ds(HEADS + g * 4, 4), rows, :].reshape(4 * SPAN, DE)
            e = jnp.exp(nt(qw, xs) * SCALE)
            probs = e / jnp.sum(e, axis=-1, keepdims=True)
            d_probs = nt(gw, xs)
            delta = jnp.sum(probs * d_probs, axis=-1, keepdims=True)
            ds = (probs * (d_probs - delta) * SCALE).astype(BF)
            pb = probs.astype(BF)
            pbuf[s, pl.ds(g * 4, 4)] = pb.reshape(4, SPAN, HS)
            dsbuf[s, pl.ds(g * 4, 4)] = ds.reshape(4, SPAN, HS)
            new = tn(ds, qw) + tn(pb, gw)
            if first:
                acc[s] = new
            else:
                acc[s] = acc[s] + new
            return 0

        lax.fori_loop(0, 2, one, 0)

    def outputs(g):
        for t, buf, out in ((0, dsbuf, dqv), (1, pbuf, attv)):
            for s in range(2):
                lhs = buf[s, pl.ds(g * 4, 4)].reshape(4 * SPAN, HS)
                px[:, s] = nn(lhs, xrd[s]).astype(BF).reshape(4, SPAN, DE)
            for i in range(4):
                h = g * 4 + i
                res = nn(px[i].reshape(2 * SPAN, DE), wbuf[t * HEADS + h])
                out[:, h * HS:(h + 1) * HS] = res.astype(BF)

    enc_start()
    stage(0)
    enc_z()
    stage(1)
    enc_1()
    stage(2)
    enc_2()
    stage(3)
    loads[2].wait()
    loads[3].wait()
    project_0_done = False
    enc_3()
    stage(4)
    stage(5)
    from_sib((0,))
    project(0)
    stage(6)
    enc_sib()
    pos = [slot_s[0, ids_s[0, s, r]] for s in range(2) for r in range(2)]
    for s in range(2):
        for r in range(2):
            p = pos[2 * s + r]
            xrd[s, r * NLEN:(r + 1) * NLEN] = encbuf[p // 2, p % 2]
    recv(("ids",), sibids_v, sib)
    cp = pltpu.make_async_copy(sibids_v, sibids_s, lsem.at[4])
    cp.start()
    cp.wait()
    stage(7)
    from_sib((-1, 1))
    project(-1)
    project(1)
    stage(8)
    from_sib((-2, 2))
    project(-2)
    stage(9)
    project(2)
    attend(2, True)
    stage(10)
    from_sib((-3, 3))
    project(-3)
    stage(11)
    project(3)
    attend(1, False)
    attend(-1, False)
    from_sib((4,))
    project(4)
    attend(0, False)

    for s in range(2):
        own16[s, 0:2] = acc[s].astype(BF).reshape(2, NLEN, DE)
        own16[s, 2] = jnp.zeros((NLEN, DE), BF)
        sib16[s, 2] = jnp.zeros((NLEN, DE), BF)
    send(2, ("rs",), own16.at[:, 0:2], sib16.at[:, 0:2], sib)
    spos = [slot_s[0, sibids_s[0, s * 2 + r]] for s in range(2) for r in range(2)]

    def which(ps, s, p):
        return jnp.where(ps[2 * s] == p, 0, jnp.where(ps[2 * s + 1] == p, 1, 2))

    def chip_sum(dx, zz, j, rows):
        p = ((x + dx + 4) % 4) * 8 + zz * 4 + 2 * c + j
        total = own16[0, which(pos, 0, p), rows].astype(F32) + own16[1, which(pos, 1, p), rows].astype(F32)
        return total + (sib16[0, which(spos, 0, p), rows].astype(F32) + sib16[1, which(spos, 1, p), rows].astype(F32))

    TOP, BOT = slice(0, 32), slice(32, 64)
    DIRS = (("r", right_x, left_x, 1, TOP, BOT), ("l", left_x, right_x, -1, BOT, TOP))

    def far(half):
        for di, (nm, to, _, sg, mine, _) in enumerate(DIRS):
            m = 0 if half == 0 else 1
            zz = 1 - zl if half == 0 else zl
            for j in range(2):
                xsend[di, m, j] = chip_sum(2, zz, j, mine).astype(BF)
            send(2, ("x", m, nm), xsend.at[di, m], xrecv.at[di, m], to)

    def near(half):
        for di, (nm, to, _, sg, _, other) in enumerate(DIRS):
            m = 2 if half == 0 else 4
            zz = 1 - zl if half == 0 else zl
            for j in range(2):
                xsend[di, m, j] = chip_sum(sg, zz, j, other).astype(BF)
            send(2, ("x", m, nm), xsend.at[di, m], xrecv.at[di, m], to)

    def near_add(half):
        for di, (nm, to, frm, sg, mine, _) in enumerate(DIRS):
            m = 3 if half == 0 else 5
            zz = 1 - zl if half == 0 else zl
            recv(("x", half, nm), xrecv.at[di, half], frm)
            for j in range(2):
                xsend[di, m, j] = (chip_sum(sg, zz, j, mine) + xrecv[di, half, j].astype(F32)).astype(BF)
            send(2, ("x", m, nm), xsend.at[di, m], xrecv.at[di, m], to)

    def total(half):
        a, b = (2, 3) if half == 0 else (4, 5)
        for di, (nm, _, frm, _, _, _) in enumerate(DIRS):
            for m in (a, b):
                recv(("x", m, nm), xrecv.at[di, m], frm)
        zz = 1 - zl if half == 0 else zl
        for j in range(2):
            top = chip_sum(0, zz, j, TOP) + xrecv[0, b, j].astype(F32) + xrecv[1, a, j].astype(F32)
            bot = chip_sum(0, zz, j, BOT) + xrecv[0, a, j].astype(F32) + xrecv[1, b, j].astype(F32)
            if half == 0:
                zsend[j, TOP] = top.astype(BF)
                zsend[j, BOT] = bot.astype(BF)
            else:
                gout[j, TOP] = top
                gout[j, BOT] = bot

    recv(("rs",), sib16.at[:, 0:2], sib)
    far(0)
    far(1)
    near(0)
    outputs(0)
    near_add(0)
    near(1)
    outputs(1)
    near_add(1)
    outputs(2)
    total(0)
    send(2, ("rz",), zsend, zrecv, inner)
    outputs(3)
    stores = [
        pltpu.make_async_copy(attv, att_hbm, lsem.at[5]),
        pltpu.make_async_copy(dqv, dq_hbm, lsem.at[6]),
    ]
    for cp in stores:
        cp.start()
    total(1)
    recv(("rz",), zrecv, inner)
    for j in range(2):
        gout[j] = gout[j] + zrecv[j].astype(F32)
    stores.append(pltpu.make_async_copy(gout, ge_hbm, lsem.at[7]))
    stores[-1].start()

    def drain(items):
        for i, src, dev in items:
            pltpu.make_async_remote_copy(src, src, ssem.at[i], rsem.at[i], device_id=dev, device_id_type=MESH).wait_send()

    drain(sent[2])

    @pl.when(c == 0)
    def _():
        drain([(i, src_like(wbuf, n), dev) for i, n, dev in plain(sent[0])])

    @pl.when(c == 1)
    def _():
        drain([(i, src_like(wbuf, n), dev) for i, n, dev in plain(sent[1])])

    for cp in stores:
        cp.wait()
    assert len(sem.at) <= NSEM, len(sem.at)


def plain(items):
    return [(i, src.shape[0], dev) for i, src, dev in items]


def src_like(wbuf, rows):
    return wbuf.at[0, pl.ds(0, rows)]


def per_device(queries, grad_out, encoded, kv_weight, neighbour_ids, slot_map):
    ids_pad = jnp.zeros((8, 128), jnp.int32).at[0, 0:4].set(neighbour_ids.reshape(4))
    anyspec = pl.BlockSpec(memory_space=pl.ANY)
    smem = pl.BlockSpec(memory_space=pltpu.SMEM)
    att, dq, ge = pl.pallas_call(
        kernel,
        out_shape=(
            jax.ShapeDtypeStruct((2 * SPAN, HEADS * HS), BF),
            jax.ShapeDtypeStruct((2 * SPAN, HEADS * HS), BF),
            jax.ShapeDtypeStruct((2, NLEN, DE), F32),
        ),
        in_specs=[anyspec, anyspec, anyspec, anyspec, smem, smem, anyspec],
        out_specs=(anyspec, anyspec, anyspec),
        scratch_shapes=[
            pltpu.VMEM((NSH, DE, HS), BF),
            pltpu.VMEM((NSEQ, 2, NLEN, DE), BF),
            pltpu.VMEM((2, 2 * SPAN, HEADS * HS), BF),
            pltpu.VMEM((NSH, 2 * SPAN, DE), BF),
            pltpu.VMEM((2, 2 * NLEN, DE), BF),
            pltpu.VMEM((2, HEADS, SPAN, HS), BF),
            pltpu.VMEM((2, HEADS, SPAN, HS), BF),
            pltpu.VMEM((2, 2 * NLEN, DE), F32),
            pltpu.VMEM((2, 3, NLEN, DE), BF),
            pltpu.VMEM((2, 3, NLEN, DE), BF),
            pltpu.VMEM((2, 6, 2, 32, DE), BF),
            pltpu.VMEM((2, 6, 2, 32, DE), BF),
            pltpu.VMEM((2, NLEN, DE), BF),
            pltpu.VMEM((2, NLEN, DE), BF),
            pltpu.VMEM((2, NLEN, DE), F32),
            pltpu.VMEM((2 * SPAN, HEADS * HS), BF),
            pltpu.VMEM((2 * SPAN, HEADS * HS), BF),
            pltpu.VMEM((4, 2, SPAN, DE), BF),
            pltpu.VMEM((8, 128), jnp.int32),
            pltpu.SMEM((8, 128), jnp.int32),
            pltpu.SemaphoreType.DMA((NSEM,)),
            pltpu.SemaphoreType.DMA((NSEM,)),
            pltpu.SemaphoreType.DMA((8,)),
        ],
        compiler_params=pltpu.CompilerParams(
            collective_id=0, has_side_effects=True, vmem_limit_bytes=56 * 1024 * 1024
        ),
    )(queries[0], grad_out[0], encoded[0], kv_weight, neighbour_ids, slot_map, ids_pad)
    return att[None], dq[None], ge[None]


def solution(mesh):
    in_specs = (
        P("dp", "seq", None),
        P("dp", "seq", None),
        P("dp", "seq", None, None),
        P(None, "dp"),
        P("dp", "seq", None),
        P("dp", None),
    )
    out_specs = (P("dp", "seq", None), P("dp", "seq", None), P("dp", "seq", None, None))
    return jax.shard_map(
        per_device, mesh=mesh, in_specs=in_specs, out_specs=out_specs, check_vma=False
    )
```

```python
import jax
import jax.numpy as jnp
from jax import lax
from jax.experimental import pallas as pl
from jax.experimental.pallas import tpu as pltpu
from jax.sharding import PartitionSpec as P

MESH = pl.DeviceIdType.MESH
BF = jnp.bfloat16
F32 = jnp.float32

HS = 128
HEADS = 16
SPAN = 64
NLEN = 64
DE = 896
NSH = 32
NSEQ = 16
CUT = 416
SCALE = HS ** -0.5


class Sems:
    def __init__(self):
        self.at = {}

    def __call__(self, *name):
        return self.at.setdefault(name, len(self.at))


def nt(a, b):
    return lax.dot_general(a, b, (((1,), (1,)), ((), ())), preferred_element_type=F32)


def tn(a, b):
    return lax.dot_general(a, b, (((0,), (0,)), ((), ())), preferred_element_type=F32)


def nn(a, b):
    return lax.dot_general(a, b, (((1,), (0,)), ((), ())), preferred_element_type=F32)


NSEM = 192


def kernel(
    q_hbm, g_hbm, enc_hbm, w_hbm, ids_s, slot_s,
    attv, dqv, gout,
    wbuf, encbuf, qg, qgw, xrd, pbuf, dsbuf, acc, own16, sib16,
    xsend, xrecv, zsend, zrecv, px, ids_v, sibids_v, sibids_s,
    ssem, rsem, lsem,
):
    dp = lax.axis_index("dp")
    sq = lax.axis_index("seq")
    y, k = dp // 4, dp % 4
    x, zl, c = sq // 4, (sq // 2) % 2, sq % 2
    o = 2 * zl - 1
    right2_y = (((y + 2) % 8) * 4 + k, sq)
    left2_y = (((y + 6) % 8) * 4 + k, sq)
    right_y = (((y + 1) % 8) * 4 + k, sq)
    left_y = (((y + 7) % 8) * 4 + k, sq)
    sq_in = sq + 2 - 4 * zl
    outer = (y * 4 + (k + o + 4) % 4, sq_in)
    out_pair = (y * 4 + (k + o + 4) % 4, sq)
    in_pair = (y * 4 + (k - o + 4) % 4, sq)
    far = (y * 4 + (k + 2) % 4, sq_in)
    inner = (dp, sq_in)
    right_x = (dp, (sq + 4) % NSEQ)
    left_x = (dp, (sq + 12) % NSEQ)
    sib = (dp, sq + 1 - 2 * c)
    sem = Sems()
    sent = {0: [], 1: [], 2: []}

    def send(who, name, src, dst, dev):
        i = sem(*name)
        pltpu.make_async_remote_copy(src, dst, ssem.at[i], rsem.at[i], device_id=dev, device_id_type=MESH).start()
        sent[who].append((i, src, dev))

    def recv(name, dst, dev):
        i = sem(*name)
        pltpu.make_async_remote_copy(dst, dst, ssem.at[i], rsem.at[i], device_id=dev, device_id_type=MESH).wait_recv()

    loads = [
        pltpu.make_async_copy(w_hbm, wbuf.at[dp], lsem.at[0]),
        pltpu.make_async_copy(enc_hbm, encbuf.at[sq], lsem.at[1]),
        pltpu.make_async_copy(q_hbm, qg.at[0], lsem.at[2]),
        pltpu.make_async_copy(g_hbm, qg.at[1], lsem.at[3]),
    ]
    for cp in loads:
        cp.start()
    barrier = pltpu.get_barrier_semaphore()
    for dev in (right_y, left_y, right2_y, left2_y, outer, far, out_pair, in_pair, inner, right_x, left_x, sib):
        pl.semaphore_signal(barrier, inc=1, device_id=dev, device_id_type=MESH)
    lane = lax.broadcasted_iota(jnp.int32, (8, 128), 1)
    ids_vec = jnp.zeros((8, 128), jnp.int32)
    for i in range(4):
        ids_vec = jnp.where(lane == i, ids_s[0, i // 2, i % 2], ids_vec)
    ids_v[...] = ids_vec
    pl.semaphore_wait(barrier, 12)

    def shard(dy, kk):
        return ((y + dy + 8) % 8) * 4 + (kk + 8) % 4

    def seq_of(dx, zz):
        return ((x + dx + 4) % 4) * 4 + zz * 2 + c

    def enc_start():
        mine = encbuf.at[sq]
        send(2, ("ez",), enc_hbm, mine, inner)
        send(2, ("ea", "r"), enc_hbm, mine, right_x)
        send(2, ("ea", "l"), enc_hbm, mine, left_x)
        send(2, ("es", 0), enc_hbm, mine, sib)
        send(2, ("ids",), ids_v, sibids_v, sib)

    def enc_z():
        ref = encbuf.at[seq_of(0, 1 - zl)]
        recv(("ez",), ref, inner)
        send(2, ("eb", "r"), ref, ref, right_x)
        send(2, ("eb", "l"), ref, ref, left_x)
        send(2, ("es", 1), ref, ref, sib)

    def enc_1():
        ref = encbuf.at[seq_of(-1, zl)]
        recv(("ea", "r"), ref, left_x)
        send(2, ("e2", "r"), ref, ref, right_x)
        send(2, ("es", 2), ref, ref, sib)
        ref = encbuf.at[seq_of(1, zl)]
        recv(("ea", "l"), ref, right_x)
        send(2, ("es", 3), ref, ref, sib)

    def enc_2():
        ref = encbuf.at[seq_of(1, 1 - zl)]
        recv(("eb", "l"), ref, right_x)
        send(2, ("e2", "l"), ref, ref, left_x)
        send(2, ("es", 4), ref, ref, sib)
        ref = encbuf.at[seq_of(-1, 1 - zl)]
        recv(("eb", "r"), ref, left_x)
        send(2, ("es", 5), ref, ref, sib)

    def enc_3():
        ref = encbuf.at[seq_of(2, zl)]
        recv(("e2", "r"), ref, left_x)
        send(2, ("es", 6), ref, ref, sib)
        ref = encbuf.at[seq_of(2, 1 - zl)]
        recv(("e2", "l"), ref, right_x)
        send(2, ("es", 7), ref, ref, sib)

    def enc_sib():
        cs = 1 - c
        for i, (dx, zz) in enumerate(((0, zl), (0, 1 - zl), (-1, zl), (1, zl), (1, 1 - zl), (-1, 1 - zl), (2, zl), (2, 1 - zl))):
            recv(("es", i), encbuf.at[((x + dx + 4) % 4) * 4 + zz * 2 + cs], sib)

    R0 = (0, CUT)
    RN = (CUT, DE - CUT)

    def part(core, half=None):
        n = RN[core]
        if half is None:
            return R0[core], n
        return pl.multiple_of(R0[core] + half * (n // 2), 16), n // 2

    def wp(d, core, half=None):
        r0, n = part(core, half)
        return wbuf.at[d, pl.ds(r0, n)]

    def own(core, half=None):
        r0, n = part(core, half)
        return w_hbm.at[pl.ds(r0, n)]

    KK = (lambda: k, lambda: k + o, lambda: k - o, lambda: k + 2)

    def to_sib(core, dy, m):
        ref = wp(shard(dy, KK[m]()), core)
        send(core, ("ws", core, dy, m), ref, ref, sib)

    OFFS = (0, -1, 1, -2, 2, -3, 3, 4)

    def y0(dy):
        d = shard(dy, k)
        mine, dst = own(0), wp(d, 0)
        if dy == 0:
            send(0, ("y2r",), mine, dst, right2_y)
            send(0, ("y2l",), mine, dst, left2_y)
            send(0, ("y1r",), mine, dst, right_y)
            send(0, ("y1l",), mine, dst, left_y)
        elif dy == -1:
            recv(("y1r",), dst, left_y)
        elif dy == 1:
            recv(("y1l",), dst, right_y)
        elif dy == -2:
            recv(("y2r",), dst, left2_y)
            send(0, ("y3r",), dst, dst, right_y)
            send(0, ("y4r",), wp(d, 0, 0), wp(d, 0, 0), right2_y)
        elif dy == 2:
            recv(("y2l",), dst, right2_y)
            send(0, ("y3l",), dst, dst, left_y)
            send(0, ("y4l",), wp(d, 0, 1), wp(d, 0, 1), left2_y)
        elif dy == -3:
            recv(("y3r",), dst, left_y)
        elif dy == 3:
            recv(("y3l",), dst, right_y)
        else:
            recv(("y4r",), wp(d, 0, 0), left2_y)
            recv(("y4l",), wp(d, 0, 1), right2_y)

    def z0_start(dy):
        d = shard(dy, k)
        src = own(0) if dy == 0 else wp(d, 0)
        half = own(0, zl) if dy == 0 else wp(d, 0, zl)
        send(0, ("zo", dy), src, wp(d, 0), outer)
        send(0, ("zf", dy), half, wp(d, 0, zl), far)

    def z0_pass(dy):
        ref = wp(shard(dy, k + o), 0)
        recv(("zo", dy), ref, outer)
        send(0, ("zi", dy), ref, ref, inner)
        to_sib(0, dy, 1)
        ref = wp(shard(dy, k + 2), 0, 1 - zl)
        recv(("zf", dy), ref, far)
        send(0, ("zh", dy), ref, ref, inner)

    def z0_last(dy):
        recv(("zi", dy), wp(shard(dy, k - o), 0), inner)
        to_sib(0, dy, 2)
        recv(("zh", dy), wp(shard(dy, k + 2), 0, zl), inner)
        to_sib(0, dy, 3)

    def core0(n):
        if n < 8:
            dy = OFFS[n]
            y0(dy)
            z0_start(dy)
            if n:
                to_sib(0, dy, 0)
        if 3 <= n <= 10:
            z0_pass(OFFS[n - 3])
        if 5 <= n <= 12:
            z0_last(OFFS[n - 5])

    def y1_start(m):
        d = shard(0, KK[m]())
        src = own(1) if m == 0 else wp(d, 1)
        send(1, ("yr", 1, m), src, wp(d, 1), right_y)
        send(1, ("yl", 1, m), src, wp(d, 1), left_y)

    def y1_pass(dy, m):
        d = shard(dy, KK[m]())
        if dy == 4:
            recv(("yr", 4, m), wp(d, 1, 0), left_y)
            recv(("yl", 4, m), wp(d, 1, 1), right_y)
        else:
            nm, to, frm, half = ("yr", right_y, left_y, 0) if dy < 0 else ("yl", left_y, right_y, 1)
            st = abs(dy)
            recv((nm, st, m), wp(d, 1), frm)
            ref = wp(d, 1) if st < 3 else wp(d, 1, half)
            send(1, (nm, st + 1, m), ref, ref, to)
        to_sib(1, dy, m)

    def both(st, m):
        if st < 4:
            y1_pass(-st, m)
            y1_pass(st, m)
        else:
            y1_pass(4, m)

    def core1(n):
        if n == 0:
            d = shard(0, k)
            send(1, ("wo",), own(1), wp(d, 1), outer)
            send(1, ("wd",), own(1), wp(d, 1), out_pair)
            send(1, ("wf",), own(1), wp(d, 1), far)
            y1_start(0)
        elif n == 2:
            for m, nm, frm in ((1, "wo", outer), (2, "wd", in_pair), (3, "wf", far)):
                recv((nm,), wp(shard(0, KK[m]()), 1), frm)
                y1_start(m)
                to_sib(1, 0, m)
        else:
            for sm in {1: ((1, 0),), 3: ((1, 1), (2, 0)), 4: ((1, 2), (1, 3)), 5: ((2, 1), (3, 0)), 6: ((2, 2), (2, 3)),
                       7: ((3, 1), (4, 0)), 8: ((3, 2), (3, 3)), 9: ((4, 1),), 10: ((4, 2),), 11: ((4, 3),), 12: ()}[n]:
                both(*sm)

    def stage(n):
        @pl.when(c == 0)
        def _():
            core0(n)

        @pl.when(c == 1)
        def _():
            core1(n)

    def from_sib(dys):
        for core in range(2):
            @pl.when(c == core)
            def _():
                for dy in dys:
                    for m in range(4):
                        if dy or m:
                            recv(("ws", 1 - core, dy, m), wp(shard(dy, KK[m]()), 1 - core), sib)

    def project(dy):
        base = ((y + dy + 8) % 8) * 4

        def one(i, _):
            d = base + i
            t = d // HEADS
            h = d % HEADS
            lhs = qg[t, :, pl.ds(pl.multiple_of(h * HS, HS), HS)]
            qgw[d] = nt(lhs, wbuf[d]).astype(BF)
            return 0

        lax.fori_loop(0, 4, one, 0, unroll=True)

    def attend(dy, first):
        g = (y + dy + 8) % 4

        def one(s, _):
            rows = pl.ds(pl.multiple_of(s * SPAN, SPAN), SPAN)
            xs = xrd[s]
            qw = qgw[pl.ds(g * 4, 4), rows, :].reshape(4 * SPAN, DE)
            gw = qgw[pl.ds(HEADS + g * 4, 4), rows, :].reshape(4 * SPAN, DE)
            e = jnp.exp(nt(qw, xs) * SCALE)
            probs = e / jnp.sum(e, axis=-1, keepdims=True)
            d_probs = nt(gw, xs)
            delta = jnp.sum(probs * d_probs, axis=-1, keepdims=True)
            ds = (probs * (d_probs - delta) * SCALE).astype(BF)
            pb = probs.astype(BF)
            pbuf[s, pl.ds(g * 4, 4)] = pb.reshape(4, SPAN, HS)
            dsbuf[s, pl.ds(g * 4, 4)] = ds.reshape(4, SPAN, HS)
            new = tn(ds, qw) + tn(pb, gw)
            if first:
                acc[s] = new
            else:
                acc[s] = acc[s] + new
            return 0

        lax.fori_loop(0, 2, one, 0, unroll=True)

    def outputs(dy):
        g = (y + dy + 8) % 4
        for t, buf, out in ((0, dsbuf, dqv), (1, pbuf, attv)):
            for s in range(2):
                lhs = buf[s, pl.ds(g * 4, 4)].reshape(4 * SPAN, HS)
                px[t, :, s] = nn(lhs, xrd[s]).astype(BF).reshape(4, SPAN, DE)
            for i in range(4):
                h = g * 4 + i
                res = nn(px[t, i].reshape(2 * SPAN, DE), wbuf[t * HEADS + h])
                out[:, pl.ds(pl.multiple_of(h * HS, HS), HS)] = res.astype(BF)

    enc_start()
    stage(0)
    stage(1)
    stage(2)
    enc_z()
    stage(3)
    enc_1()
    for cp in loads:
        cp.wait()
    stage(4)
    stage(5)
    from_sib((0,))
    project(0)
    stage(6)
    enc_2()
    stage(7)
    from_sib((-1, 1))
    project(-1)
    project(1)
    stage(8)
    enc_3()
    stage(9)
    from_sib((-2, 2))
    project(-2)
    project(2)
    enc_sib()
    pos = [slot_s[0, ids_s[0, s, r]] for s in range(2) for r in range(2)]
    for s in range(2):
        for r in range(2):
            p = pos[2 * s + r]
            xrd[s, r * NLEN:(r + 1) * NLEN] = encbuf[p // 2, p % 2]
    stage(10)
    recv(("ids",), sibids_v, sib)
    cp = pltpu.make_async_copy(sibids_v, sibids_s, lsem.at[4])
    cp.start()
    attend(2, True)
    from_sib((-3,))
    project(-3)
    attend(1, False)
    outputs(2)
    cp.wait()
    stage(11)
    from_sib((3,))
    project(3)
    attend(-1, False)
    stage(12)
    from_sib((4,))
    project(4)
    attend(0, False)

    for s in range(2):
        own16[s, 0:2] = acc[s].astype(BF).reshape(2, NLEN, DE)
        own16[s, 2] = jnp.zeros((NLEN, DE), BF)
        sib16[s, 2] = jnp.zeros((NLEN, DE), BF)
    send(2, ("rs",), own16.at[:, 0:2], sib16.at[:, 0:2], sib)
    spos = [slot_s[0, sibids_s[0, s * 2 + r]] for s in range(2) for r in range(2)]

    def which(ps, s, p):
        return jnp.where(ps[2 * s] == p, 0, jnp.where(ps[2 * s + 1] == p, 1, 2))

    def chip_sum(dx, zz, j, rows):
        p = ((x + dx + 4) % 4) * 8 + zz * 4 + 2 * c + j
        total = own16[0, which(pos, 0, p), rows].astype(F32) + own16[1, which(pos, 1, p), rows].astype(F32)
        return total + (sib16[0, which(spos, 0, p), rows].astype(F32) + sib16[1, which(spos, 1, p), rows].astype(F32))

    TOP, BOT = slice(0, 32), slice(32, 64)
    DIRS = (("r", right_x, left_x, 1, TOP, BOT), ("l", left_x, right_x, -1, BOT, TOP))

    def far(half):
        for di, (nm, to, _, sg, mine, _) in enumerate(DIRS):
            m = 0 if half == 0 else 1
            zz = 1 - zl if half == 0 else zl
            for j in range(2):
                xsend[di, m, j] = chip_sum(2, zz, j, mine).astype(BF)
            send(2, ("x", m, nm), xsend.at[di, m], xrecv.at[di, m], to)

    def near(half):
        for di, (nm, to, _, sg, _, other) in enumerate(DIRS):
            m = 2 if half == 0 else 4
            zz = 1 - zl if half == 0 else zl
            for j in range(2):
                xsend[di, m, j] = chip_sum(sg, zz, j, other).astype(BF)
            send(2, ("x", m, nm), xsend.at[di, m], xrecv.at[di, m], to)

    def near_add(half):
        for di, (nm, to, frm, sg, mine, _) in enumerate(DIRS):
            m = 3 if half == 0 else 5
            zz = 1 - zl if half == 0 else zl
            recv(("x", half, nm), xrecv.at[di, half], frm)
            for j in range(2):
                xsend[di, m, j] = (chip_sum(sg, zz, j, mine) + xrecv[di, half, j].astype(F32)).astype(BF)
            send(2, ("x", m, nm), xsend.at[di, m], xrecv.at[di, m], to)

    def total(half):
        a, b = (2, 3) if half == 0 else (4, 5)
        for di, (nm, _, frm, _, _, _) in enumerate(DIRS):
            for m in (a, b):
                recv(("x", m, nm), xrecv.at[di, m], frm)
        zz = 1 - zl if half == 0 else zl
        for j in range(2):
            top = chip_sum(0, zz, j, TOP) + xrecv[0, b, j].astype(F32) + xrecv[1, a, j].astype(F32)
            bot = chip_sum(0, zz, j, BOT) + xrecv[0, a, j].astype(F32) + xrecv[1, b, j].astype(F32)
            if half == 0:
                zsend[j, TOP] = top.astype(BF)
                zsend[j, BOT] = bot.astype(BF)
            else:
                gout[j, TOP] = top
                gout[j, BOT] = bot

    outputs(1)
    recv(("rs",), sib16.at[:, 0:2], sib)
    far(0)
    near(0)
    far(1)
    outputs(-1)
    near_add(0)
    near(1)
    near_add(1)
    outputs(0)
    total(0)
    send(2, ("rz",), zsend, zrecv, inner)
    total(1)
    recv(("rz",), zrecv, inner)
    for j in range(2):
        gout[j] = gout[j] + zrecv[j].astype(F32)

    def drain(items):
        for i, src, dev in items:
            pltpu.make_async_remote_copy(src, src, ssem.at[i], rsem.at[i], device_id=dev, device_id_type=MESH).wait_send()

    drain(sent[2])
    rows_sent = [[(i, src.shape[0], dev) for i, src, dev in sent[core]] for core in range(2)]

    for core in range(2):
        @pl.when(c == core)
        def _():
            drain([(i, wbuf.at[0, pl.ds(0, n)], dev) for i, n, dev in rows_sent[core]])

    assert len(sem.at) <= NSEM, len(sem.at)


def per_device(queries, grad_out, encoded, kv_weight, neighbour_ids, slot_map):
    anyspec = pl.BlockSpec(memory_space=pltpu.HBM)
    smem = pl.BlockSpec(memory_space=pltpu.SMEM)
    vmem = pl.BlockSpec(memory_space=pltpu.VMEM)
    att, dq, ge = pl.pallas_call(
        kernel,
        out_shape=(
            pltpu.VMEM((2 * SPAN, HEADS * HS), BF),
            pltpu.VMEM((2 * SPAN, HEADS * HS), BF),
            pltpu.VMEM((2, NLEN, DE), F32),
        ),
        in_specs=[anyspec, anyspec, anyspec, anyspec, smem, smem],
        out_specs=(vmem, vmem, vmem),
        scratch_shapes=[
            pltpu.VMEM((NSH, DE, HS), BF),
            pltpu.VMEM((NSEQ, 2, NLEN, DE), BF),
            pltpu.VMEM((2, 2 * SPAN, HEADS * HS), BF),
            pltpu.VMEM((NSH, 2 * SPAN, DE), BF),
            pltpu.VMEM((2, 2 * NLEN, DE), BF),
            pltpu.VMEM((2, HEADS, SPAN, HS), BF),
            pltpu.VMEM((2, HEADS, SPAN, HS), BF),
            pltpu.VMEM((2, 2 * NLEN, DE), F32),
            pltpu.VMEM((2, 3, NLEN, DE), BF),
            pltpu.VMEM((2, 3, NLEN, DE), BF),
            pltpu.VMEM((2, 6, 2, 32, DE), BF),
            pltpu.VMEM((2, 6, 2, 32, DE), BF),
            pltpu.VMEM((2, NLEN, DE), BF),
            pltpu.VMEM((2, NLEN, DE), BF),
            pltpu.VMEM((2, 4, 2, SPAN, DE), BF),
            pltpu.VMEM((8, 128), jnp.int32),
            pltpu.VMEM((8, 128), jnp.int32),
            pltpu.SMEM((8, 128), jnp.int32),
            pltpu.SemaphoreType.DMA((NSEM,)),
            pltpu.SemaphoreType.DMA((NSEM,)),
            pltpu.SemaphoreType.DMA((8,)),
        ],
        compiler_params=pltpu.CompilerParams(
            collective_id=0, has_side_effects=True, vmem_limit_bytes=58 * 1024 * 1024
        ),
    )(queries[0], grad_out[0], encoded[0], kv_weight, neighbour_ids, slot_map)
    return att[None], dq[None], ge[None]


def solution(mesh):
    in_specs = (
        P("dp", "seq", None),
        P("dp", "seq", None),
        P("dp", "seq", None, None),
        P(None, "dp"),
        P("dp", "seq", None),
        P("dp", None),
    )
    out_specs = (P("dp", "seq", None), P("dp", "seq", None), P("dp", "seq", None, None))
    return jax.shard_map(
        per_device, mesh=mesh, in_specs=in_specs, out_specs=out_specs, check_vma=False
    )
```

```python
import jax
import jax.numpy as jnp
from jax import lax
from jax.experimental import pallas as pl
from jax.experimental.pallas import tpu as pltpu
from jax.sharding import PartitionSpec as P

MESH = pl.DeviceIdType.MESH
BF = jnp.bfloat16
F32 = jnp.float32

HS = 128
HEADS = 16
SPAN = 64
NLEN = 64
DE = 896
NSH = 32
NSEQ = 16
CUT = 416
SCALE = HS ** -0.5


class Sems:
    def __init__(self):
        self.at = {}

    def __call__(self, *name):
        return self.at.setdefault(name, len(self.at))


def nt(a, b):
    return lax.dot_general(a, b, (((1,), (1,)), ((), ())), preferred_element_type=F32)


def tn(a, b):
    return lax.dot_general(a, b, (((0,), (0,)), ((), ())), preferred_element_type=F32)


def nn(a, b):
    return lax.dot_general(a, b, (((1,), (0,)), ((), ())), preferred_element_type=F32)


NSEM = 208


def kernel(
    q_hbm, g_hbm, enc_hbm, w_hbm, ids_s, slot_s,
    attv, dqv, gout,
    wbuf, encbuf, qg, qgw, xrd, pbuf, dsbuf, acc, own16, sib16,
    xsend, xrecv, zsend, zrecv, bzs, bzr, bfs, bfr, bns, bnr, px, ids_v, sibids_v, sibids_s,
    ssem, rsem, lsem,
):
    dp = lax.axis_index("dp")
    sq = lax.axis_index("seq")
    y, k = dp // 4, dp % 4
    x, zl, c = sq // 4, (sq // 2) % 2, sq % 2
    o = 2 * zl - 1
    right2_y = (((y + 2) % 8) * 4 + k, sq)
    left2_y = (((y + 6) % 8) * 4 + k, sq)
    right_y = (((y + 1) % 8) * 4 + k, sq)
    left_y = (((y + 7) % 8) * 4 + k, sq)
    sq_in = sq + 2 - 4 * zl
    outer = (y * 4 + (k + o + 4) % 4, sq_in)
    out_pair = (y * 4 + (k + o + 4) % 4, sq)
    in_pair = (y * 4 + (k - o + 4) % 4, sq)
    far = (y * 4 + (k + 2) % 4, sq_in)
    inner = (dp, sq_in)
    right_x = (dp, (sq + 4) % NSEQ)
    left_x = (dp, (sq + 12) % NSEQ)
    sib = (dp, sq + 1 - 2 * c)
    sem = Sems()
    sent = {0: [], 1: [], 2: []}

    def send(who, name, src, dst, dev):
        i = sem(*name)
        pltpu.make_async_remote_copy(src, dst, ssem.at[i], rsem.at[i], device_id=dev, device_id_type=MESH).start()
        sent[who].append((i, src, dev))

    def recv(name, dst, dev):
        i = sem(*name)
        pltpu.make_async_remote_copy(dst, dst, ssem.at[i], rsem.at[i], device_id=dev, device_id_type=MESH).wait_recv()

    loads = [
        pltpu.make_async_copy(w_hbm, wbuf.at[dp], lsem.at[0]),
        pltpu.make_async_copy(enc_hbm, encbuf.at[sq], lsem.at[1]),
        pltpu.make_async_copy(q_hbm, qg.at[0], lsem.at[2]),
        pltpu.make_async_copy(g_hbm, qg.at[1], lsem.at[3]),
    ]
    for cp in loads:
        cp.start()
    barrier = pltpu.get_barrier_semaphore()
    for dev in (right_y, left_y, right2_y, left2_y, outer, far, out_pair, in_pair, inner, right_x, left_x, sib):
        pl.semaphore_signal(barrier, inc=1, device_id=dev, device_id_type=MESH)
    lane = lax.broadcasted_iota(jnp.int32, (8, 128), 1)
    ids_vec = jnp.zeros((8, 128), jnp.int32)
    for i in range(4):
        ids_vec = jnp.where(lane == i, ids_s[0, i // 2, i % 2], ids_vec)
    ids_v[...] = ids_vec
    pl.semaphore_wait(barrier, 12)

    def shard(dy, kk):
        return ((y + dy + 8) % 8) * 4 + (kk + 8) % 4

    def seq_of(dx, zz):
        return ((x + dx + 4) % 4) * 4 + zz * 2 + c

    def enc_start():
        mine = encbuf.at[sq]
        send(2, ("ez",), enc_hbm, mine, inner)
        send(2, ("ea", "r"), enc_hbm, mine, right_x)
        send(2, ("ea", "l"), enc_hbm, mine, left_x)
        send(2, ("es", 0), enc_hbm, mine, sib)
        send(2, ("ids",), ids_v, sibids_v, sib)

    def enc_z():
        ref = encbuf.at[seq_of(0, 1 - zl)]
        recv(("ez",), ref, inner)
        send(2, ("eb", "r"), ref, ref, right_x)
        send(2, ("eb", "l"), ref, ref, left_x)
        send(2, ("es", 1), ref, ref, sib)

    def enc_1():
        ref = encbuf.at[seq_of(-1, zl)]
        recv(("ea", "r"), ref, left_x)
        send(2, ("e2", "r"), ref, ref, right_x)
        send(2, ("es", 2), ref, ref, sib)
        ref = encbuf.at[seq_of(1, zl)]
        recv(("ea", "l"), ref, right_x)
        send(2, ("es", 3), ref, ref, sib)

    def enc_2():
        ref = encbuf.at[seq_of(1, 1 - zl)]
        recv(("eb", "l"), ref, right_x)
        send(2, ("e2", "l"), ref, ref, left_x)
        send(2, ("es", 4), ref, ref, sib)
        ref = encbuf.at[seq_of(-1, 1 - zl)]
        recv(("eb", "r"), ref, left_x)
        send(2, ("es", 5), ref, ref, sib)

    def enc_3():
        ref = encbuf.at[seq_of(2, zl)]
        recv(("e2", "r"), ref, left_x)
        send(2, ("es", 6), ref, ref, sib)
        ref = encbuf.at[seq_of(2, 1 - zl)]
        recv(("e2", "l"), ref, right_x)
        send(2, ("es", 7), ref, ref, sib)

    def enc_sib():
        cs = 1 - c
        for i, (dx, zz) in enumerate(((0, zl), (0, 1 - zl), (-1, zl), (1, zl), (1, 1 - zl), (-1, 1 - zl), (2, zl), (2, 1 - zl))):
            recv(("es", i), encbuf.at[((x + dx + 4) % 4) * 4 + zz * 2 + cs], sib)

    R0 = (0, CUT)
    RN = (CUT, DE - CUT)

    def part(core, half=None):
        n = RN[core]
        if half is None:
            return R0[core], n
        return pl.multiple_of(R0[core] + half * (n // 2), 16), n // 2

    def wp(d, core, half=None):
        r0, n = part(core, half)
        return wbuf.at[d, pl.ds(r0, n)]

    def own(core, half=None):
        r0, n = part(core, half)
        return w_hbm.at[pl.ds(r0, n)]

    KK = (lambda: k, lambda: k + o, lambda: k - o, lambda: k + 2)

    def to_sib(core, dy, m):
        ref = wp(shard(dy, KK[m]()), core)
        send(core, ("ws", core, dy, m), ref, ref, sib)

    OFFS = (0, -1, 1, -2, 2, -3, 3, 4)

    def y0(dy):
        d = shard(dy, k)
        mine, dst = own(0), wp(d, 0)
        if dy == 0:
            send(0, ("y2r",), mine, dst, right2_y)
            send(0, ("y2l",), mine, dst, left2_y)
            send(0, ("y1r",), mine, dst, right_y)
            send(0, ("y1l",), mine, dst, left_y)
        elif dy == -1:
            recv(("y1r",), dst, left_y)
        elif dy == 1:
            recv(("y1l",), dst, right_y)
        elif dy == -2:
            recv(("y2r",), dst, left2_y)
            send(0, ("y3r",), dst, dst, right_y)
            send(0, ("y4r",), wp(d, 0, 0), wp(d, 0, 0), right2_y)
        elif dy == 2:
            recv(("y2l",), dst, right2_y)
            send(0, ("y3l",), dst, dst, left_y)
            send(0, ("y4l",), wp(d, 0, 1), wp(d, 0, 1), left2_y)
        elif dy == -3:
            recv(("y3r",), dst, left_y)
        elif dy == 3:
            recv(("y3l",), dst, right_y)
        else:
            recv(("y4r",), wp(d, 0, 0), left2_y)
            recv(("y4l",), wp(d, 0, 1), right2_y)

    def z0_start(dy):
        d = shard(dy, k)
        src = own(0) if dy == 0 else wp(d, 0)
        half = own(0, zl) if dy == 0 else wp(d, 0, zl)
        send(0, ("zo", dy), src, wp(d, 0), outer)
        send(0, ("zf", dy), half, wp(d, 0, zl), far)

    def z0_pass(dy):
        ref = wp(shard(dy, k + o), 0)
        recv(("zo", dy), ref, outer)
        send(0, ("zi", dy), ref, ref, inner)
        to_sib(0, dy, 1)
        ref = wp(shard(dy, k + 2), 0, 1 - zl)
        recv(("zf", dy), ref, far)
        send(0, ("zh", dy), ref, ref, inner)

    def z0_last(dy):
        recv(("zi", dy), wp(shard(dy, k - o), 0), inner)
        to_sib(0, dy, 2)
        recv(("zh", dy), wp(shard(dy, k + 2), 0, zl), inner)
        to_sib(0, dy, 3)

    def core0(n):
        if n < 8:
            dy = OFFS[n]
            y0(dy)
            z0_start(dy)
            if n:
                to_sib(0, dy, 0)
        if 3 <= n <= 10:
            z0_pass(OFFS[n - 3])
        if 5 <= n <= 12:
            z0_last(OFFS[n - 5])

    def y1_start(m):
        d = shard(0, KK[m]())
        src = own(1) if m == 0 else wp(d, 1)
        send(1, ("yr", 1, m), src, wp(d, 1), right_y)
        send(1, ("yl", 1, m), src, wp(d, 1), left_y)

    def y1_pass(dy, m):
        d = shard(dy, KK[m]())
        if dy == 4:
            recv(("yr", 4, m), wp(d, 1, 0), left_y)
            recv(("yl", 4, m), wp(d, 1, 1), right_y)
        else:
            nm, to, frm, half = ("yr", right_y, left_y, 0) if dy < 0 else ("yl", left_y, right_y, 1)
            st = abs(dy)
            recv((nm, st, m), wp(d, 1), frm)
            ref = wp(d, 1) if st < 3 else wp(d, 1, half)
            send(1, (nm, st + 1, m), ref, ref, to)
        to_sib(1, dy, m)

    def both(st, m):
        if st < 4:
            y1_pass(-st, m)
            y1_pass(st, m)
        else:
            y1_pass(4, m)

    def core1(n):
        if n == 0:
            d = shard(0, k)
            send(1, ("wo",), own(1), wp(d, 1), outer)
            send(1, ("wd",), own(1), wp(d, 1), out_pair)
            send(1, ("wf",), own(1), wp(d, 1), far)
            y1_start(0)
        elif n == 2:
            for m, nm, frm in ((1, "wo", outer), (2, "wd", in_pair), (3, "wf", far)):
                recv((nm,), wp(shard(0, KK[m]()), 1), frm)
                y1_start(m)
                to_sib(1, 0, m)
        else:
            for sm in {1: ((1, 0),), 3: ((1, 1), (2, 0)), 4: ((1, 2), (1, 3)), 5: ((2, 1), (3, 0)), 6: ((2, 2), (2, 3)),
                       7: ((3, 1), (4, 0)), 8: ((3, 2), (3, 3)), 9: ((4, 1),), 10: ((4, 2),), 11: ((4, 3),), 12: ()}[n]:
                both(*sm)

    def stage(n):
        @pl.when(c == 0)
        def _():
            core0(n)

        @pl.when(c == 1)
        def _():
            core1(n)

    def from_sib(dys):
        for core in range(2):
            @pl.when(c == core)
            def _():
                for dy in dys:
                    for m in range(4):
                        if dy or m:
                            recv(("ws", 1 - core, dy, m), wp(shard(dy, KK[m]()), 1 - core), sib)

    def project(dy):
        base = ((y + dy + 8) % 8) * 4

        def one(i, _):
            d = base + i
            t = d // HEADS
            h = d % HEADS
            lhs = qg[t, :, pl.ds(pl.multiple_of(h * HS, HS), HS)]
            qgw[d] = nt(lhs, wbuf[d]).astype(BF)
            return 0

        lax.fori_loop(0, 4, one, 0, unroll=True)

    def attend(dy, first):
        g = (y + dy + 8) % 4

        def one(s, _):
            rows = pl.ds(pl.multiple_of(s * SPAN, SPAN), SPAN)
            xs = xrd[s]
            qw = qgw[pl.ds(g * 4, 4), rows, :].reshape(4 * SPAN, DE)
            gw = qgw[pl.ds(HEADS + g * 4, 4), rows, :].reshape(4 * SPAN, DE)
            e = jnp.exp(nt(qw, xs) * SCALE)
            probs = e / jnp.sum(e, axis=-1, keepdims=True)
            d_probs = nt(gw, xs)
            delta = jnp.sum(probs * d_probs, axis=-1, keepdims=True)
            ds = (probs * (d_probs - delta) * SCALE).astype(BF)
            pb = probs.astype(BF)
            pbuf[s, pl.ds(g * 4, 4)] = pb.reshape(4, SPAN, HS)
            dsbuf[s, pl.ds(g * 4, 4)] = ds.reshape(4, SPAN, HS)
            new = tn(ds, qw) + tn(pb, gw)
            if first:
                acc[s] = new
            else:
                acc[s] = acc[s] + new
            return 0

        lax.fori_loop(0, 2, one, 0, unroll=True)

    def outputs(dy):
        g = (y + dy + 8) % 4
        for t, buf, out in ((0, dsbuf, dqv), (1, pbuf, attv)):
            for s in range(2):
                lhs = buf[s, pl.ds(g * 4, 4)].reshape(4 * SPAN, HS)
                px[t, :, s] = nn(lhs, xrd[s]).astype(BF).reshape(4, SPAN, DE)
            for i in range(4):
                h = g * 4 + i
                res = nn(px[t, i].reshape(2 * SPAN, DE), wbuf[t * HEADS + h])
                out[:, pl.ds(pl.multiple_of(h * HS, HS), HS)] = res.astype(BF)

    enc_start()
    stage(0)
    stage(1)
    stage(2)
    enc_z()
    stage(3)
    enc_1()
    for cp in loads:
        cp.wait()
    stage(4)
    stage(5)
    from_sib((0,))
    project(0)
    stage(6)
    enc_2()
    stage(7)
    from_sib((-1, 1))
    project(-1)
    project(1)
    stage(8)
    enc_3()
    stage(9)
    from_sib((-2, 2))
    project(-2)
    project(2)
    enc_sib()
    pos = [slot_s[0, ids_s[0, s, r]] for s in range(2) for r in range(2)]
    for s in range(2):
        for r in range(2):
            p = pos[2 * s + r]
            xrd[s, r * NLEN:(r + 1) * NLEN] = encbuf[p // 2, p % 2]
    stage(10)
    recv(("ids",), sibids_v, sib)
    cp = pltpu.make_async_copy(sibids_v, sibids_s, lsem.at[4])
    cp.start()
    attend(2, True)
    from_sib((-3,))
    project(-3)
    attend(1, False)
    outputs(2)
    cp.wait()
    stage(11)
    from_sib((3,))
    project(3)
    attend(-1, False)
    stage(12)
    from_sib((4,))
    project(4)
    attend(0, False)

    for s in range(2):
        own16[s, 0:2] = acc[s].astype(BF).reshape(2, NLEN, DE)
        own16[s, 2] = jnp.zeros((NLEN, DE), BF)
        sib16[s, 2] = jnp.zeros((NLEN, DE), BF)
    send(2, ("rs",), own16.at[:, 0:2], sib16.at[:, 0:2], sib)
    spos = [slot_s[0, sibids_s[0, s * 2 + r]] for s in range(2) for r in range(2)]

    def which(ps, s, p):
        return jnp.where(ps[2 * s] == p, 0, jnp.where(ps[2 * s + 1] == p, 1, 2))

    def chip_sum(dx, zz, j, rows):
        p = ((x + dx + 4) % 4) * 8 + zz * 4 + 2 * c + j
        total = own16[0, which(pos, 0, p), rows].astype(F32) + own16[1, which(pos, 1, p), rows].astype(F32)
        return total + (sib16[0, which(spos, 0, p), rows].astype(F32) + sib16[1, which(spos, 1, p), rows].astype(F32))

    NA = NLEN // 2
    TOP, BOT, ROWB = slice(0, NA // 2), slice(NA // 2, NA), slice(NA, NLEN)
    DIRS = (("r", right_x, left_x, 1, TOP, BOT), ("l", left_x, right_x, -1, BOT, TOP))

    def far(half):
        for di, (nm, to, _, sg, mine, _) in enumerate(DIRS):
            zz = 1 - zl if half == 0 else zl
            for j in range(2):
                xsend[di, half, j] = chip_sum(2, zz, j, mine).astype(BF)
            send(2, ("x", half, nm), xsend.at[di, half], xrecv.at[di, half], to)

    def near(half):
        for di, (nm, to, _, sg, _, other) in enumerate(DIRS):
            m = 2 if half == 0 else 4
            zz = 1 - zl if half == 0 else zl
            for j in range(2):
                xsend[di, m, j] = chip_sum(sg, zz, j, other).astype(BF)
            send(2, ("x", m, nm), xsend.at[di, m], xrecv.at[di, m], to)

    def near_add(half):
        for di, (nm, to, frm, sg, mine, _) in enumerate(DIRS):
            m = 3 if half == 0 else 5
            zz = 1 - zl if half == 0 else zl
            recv(("x", half, nm), xrecv.at[di, half], frm)
            for j in range(2):
                xsend[di, m, j] = (chip_sum(sg, zz, j, mine) + xrecv[di, half, j].astype(F32)).astype(BF)
            send(2, ("x", m, nm), xsend.at[di, m], xrecv.at[di, m], to)

    def total(half):
        a, b = (2, 3) if half == 0 else (4, 5)
        for di, (nm, _, frm, _, _, _) in enumerate(DIRS):
            for m in (a, b):
                recv(("x", m, nm), xrecv.at[di, m], frm)
        zz = 1 - zl if half == 0 else zl
        for j in range(2):
            top = chip_sum(0, zz, j, TOP) + xrecv[0, b, j].astype(F32) + xrecv[1, a, j].astype(F32)
            bot = chip_sum(0, zz, j, BOT) + xrecv[0, a, j].astype(F32) + xrecv[1, b, j].astype(F32)
            if half == 0:
                zsend[j, TOP] = top.astype(BF)
                zsend[j, BOT] = bot.astype(BF)
            else:
                gout[j, TOP] = top
                gout[j, BOT] = bot

    COLS = (2, 1, -1, 0)

    def b_z(i):
        for j in range(2):
            bzs[i, j] = chip_sum(COLS[i], 1 - zl, j, ROWB).astype(BF)
        send(2, ("bz", i), bzs.at[i], bzr.at[i], inner)

    def b_sum(i, j):
        return chip_sum(COLS[i], zl, j, ROWB) + bzr[i, j].astype(F32)

    def b_far():
        recv(("bz", 0), bzr.at[0], inner)
        for di, (nm, to, _, _, _, _) in enumerate(DIRS):
            bfs[di] = b_sum(0, di).astype(BF)
            send(2, ("bf", nm), bfs.at[di], bfr.at[di], to)

    def b_near():
        for di, (nm, to, _, _, _, _) in enumerate(DIRS):
            recv(("bz", 1 + di), bzr.at[1 + di], inner)
            bns[di, 1 - di] = b_sum(1 + di, 1 - di).astype(BF)
            send(2, ("bn", nm, 0), bns.at[di, 1 - di], bnr.at[di, 1 - di], to)

    def b_near_add():
        for di, (nm, to, frm, _, _, _) in enumerate(DIRS):
            recv(("bf", nm), bfr.at[di], frm)
            bns[di, di] = (b_sum(1 + di, di) + bfr[di].astype(F32)).astype(BF)
            send(2, ("bn", nm, 1), bns.at[di, di], bnr.at[di, di], to)

    def b_total():
        recv(("bz", 3), bzr.at[3], inner)
        for di, (nm, _, frm, _, _, _) in enumerate(DIRS):
            recv(("bn", nm, 0), bnr.at[di, 1 - di], frm)
            recv(("bn", nm, 1), bnr.at[di, di], frm)
        for j in range(2):
            gout[j, ROWB] = b_sum(3, j) + bnr[0, j].astype(F32) + bnr[1, j].astype(F32)

    outputs(1)
    recv(("rs",), sib16.at[:, 0:2], sib)
    far(0)
    b_z(0)
    far(1)
    b_z(1)
    b_z(2)
    near(0)
    b_z(3)
    outputs(-1)
    near_add(0)
    near(1)
    b_far()
    near_add(1)
    b_near()
    b_near_add()
    total(0)
    send(2, ("rz",), zsend, zrecv, inner)
    outputs(0)
    total(1)
    b_total()
    recv(("rz",), zrecv, inner)
    for j in range(2):
        gout[j, 0:NA] = gout[j, 0:NA] + zrecv[j].astype(F32)

    def drain(items):
        for i, src, dev in items:
            pltpu.make_async_remote_copy(src, src, ssem.at[i], rsem.at[i], device_id=dev, device_id_type=MESH).wait_send()

    drain(sent[2])
    rows_sent = [[(i, src.shape[0], dev) for i, src, dev in sent[core]] for core in range(2)]

    for core in range(2):
        @pl.when(c == core)
        def _():
            drain([(i, wbuf.at[0, pl.ds(0, n)], dev) for i, n, dev in rows_sent[core]])

    assert len(sem.at) <= NSEM, len(sem.at)


def per_device(queries, grad_out, encoded, kv_weight, neighbour_ids, slot_map):
    anyspec = pl.BlockSpec(memory_space=pltpu.HBM)
    smem = pl.BlockSpec(memory_space=pltpu.SMEM)
    vmem = pl.BlockSpec(memory_space=pltpu.VMEM)
    att, dq, ge = pl.pallas_call(
        kernel,
        out_shape=(
            pltpu.VMEM((2 * SPAN, HEADS * HS), BF),
            pltpu.VMEM((2 * SPAN, HEADS * HS), BF),
            pltpu.VMEM((2, NLEN, DE), F32),
        ),
        in_specs=[anyspec, anyspec, anyspec, anyspec, smem, smem],
        out_specs=(vmem, vmem, vmem),
        scratch_shapes=[
            pltpu.VMEM((NSH, DE, HS), BF),
            pltpu.VMEM((NSEQ, 2, NLEN, DE), BF),
            pltpu.VMEM((2, 2 * SPAN, HEADS * HS), BF),
            pltpu.VMEM((NSH, 2 * SPAN, DE), BF),
            pltpu.VMEM((2, 2 * NLEN, DE), BF),
            pltpu.VMEM((2, HEADS, SPAN, HS), BF),
            pltpu.VMEM((2, HEADS, SPAN, HS), BF),
            pltpu.VMEM((2, 2 * NLEN, DE), F32),
            pltpu.VMEM((2, 3, NLEN, DE), BF),
            pltpu.VMEM((2, 3, NLEN, DE), BF),
            pltpu.VMEM((2, 6, 2, NLEN // 4, DE), BF),
            pltpu.VMEM((2, 6, 2, NLEN // 4, DE), BF),
            pltpu.VMEM((2, NLEN // 2, DE), BF),
            pltpu.VMEM((2, NLEN // 2, DE), BF),
            pltpu.VMEM((4, 2, NLEN // 2, DE), BF),
            pltpu.VMEM((4, 2, NLEN // 2, DE), BF),
            pltpu.VMEM((2, NLEN // 2, DE), BF),
            pltpu.VMEM((2, NLEN // 2, DE), BF),
            pltpu.VMEM((2, 2, NLEN // 2, DE), BF),
            pltpu.VMEM((2, 2, NLEN // 2, DE), BF),
            pltpu.VMEM((2, 4, 2, SPAN, DE), BF),
            pltpu.VMEM((8, 128), jnp.int32),
            pltpu.VMEM((8, 128), jnp.int32),
            pltpu.SMEM((8, 128), jnp.int32),
            pltpu.SemaphoreType.DMA((NSEM,)),
            pltpu.SemaphoreType.DMA((NSEM,)),
            pltpu.SemaphoreType.DMA((8,)),
        ],
        compiler_params=pltpu.CompilerParams(
            collective_id=0, has_side_effects=True, vmem_limit_bytes=58 * 1024 * 1024
        ),
    )(queries[0], grad_out[0], encoded[0], kv_weight, neighbour_ids, slot_map)
    return att[None], dq[None], ge[None]


def solution(mesh):
    in_specs = (
        P("dp", "seq", None),
        P("dp", "seq", None),
        P("dp", "seq", None, None),
        P(None, "dp"),
        P("dp", "seq", None),
        P("dp", None),
    )
    out_specs = (P("dp", "seq", None), P("dp", "seq", None), P("dp", "seq", None, None))
    return jax.shard_map(
        per_device, mesh=mesh, in_specs=in_specs, out_specs=out_specs, check_vma=False
    )
```

```python
import jax
import jax.numpy as jnp
from jax import lax
from jax.experimental import pallas as pl
from jax.experimental.pallas import tpu as pltpu
from jax.sharding import PartitionSpec as P

MESH = pl.DeviceIdType.MESH
BF = jnp.bfloat16
F32 = jnp.float32

HS = 128
HEADS = 16
SPAN = 64
NLEN = 64
DE = 896
NSH = 32
NSEQ = 16
CUT = 416
SCALE = HS ** -0.5


class Sems:
    def __init__(self):
        self.at = {}

    def __call__(self, *name):
        return self.at.setdefault(name, len(self.at))


def nt(a, b):
    return lax.dot_general(a, b, (((1,), (1,)), ((), ())), preferred_element_type=F32)


def tn(a, b):
    return lax.dot_general(a, b, (((0,), (0,)), ((), ())), preferred_element_type=F32)


def nn(a, b):
    return lax.dot_general(a, b, (((1,), (0,)), ((), ())), preferred_element_type=F32)


NSEM = 208


def kernel(
    q_hbm, g_hbm, enc_hbm, w_hbm, ids_s, slot_s,
    attv, dqv, gout,
    wbuf, encbuf, qg, qgw, xrd, pbuf, dsbuf, acc, own16, sib16,
    xsend, xrecv, zsend, zrecv, bzs, bzr, bfs, bfr, bns, bnr, px, ids_v, sibids_v, sibids_s,
    ssem, rsem, lsem,
):
    dp = lax.axis_index("dp")
    sq = lax.axis_index("seq")
    y, k = dp // 4, dp % 4
    x, zl, c = sq // 4, (sq // 2) % 2, sq % 2
    o = 2 * zl - 1
    right2_y = (((y + 2) % 8) * 4 + k, sq)
    left2_y = (((y + 6) % 8) * 4 + k, sq)
    right_y = (((y + 1) % 8) * 4 + k, sq)
    left_y = (((y + 7) % 8) * 4 + k, sq)
    sq_in = sq + 2 - 4 * zl
    outer = (y * 4 + (k + o + 4) % 4, sq_in)
    out_pair = (y * 4 + (k + o + 4) % 4, sq)
    in_pair = (y * 4 + (k - o + 4) % 4, sq)
    far = (y * 4 + (k + 2) % 4, sq_in)
    inner = (dp, sq_in)
    right_x = (dp, (sq + 4) % NSEQ)
    left_x = (dp, (sq + 12) % NSEQ)
    sib = (dp, sq + 1 - 2 * c)
    sem = Sems()
    sent = {0: [], 1: [], 2: []}

    def send(who, name, src, dst, dev):
        i = sem(*name)
        pltpu.make_async_remote_copy(src, dst, ssem.at[i], rsem.at[i], device_id=dev, device_id_type=MESH).start()
        sent[who].append((i, src, dev))

    def recv(name, dst, dev):
        i = sem(*name)
        pltpu.make_async_remote_copy(dst, dst, ssem.at[i], rsem.at[i], device_id=dev, device_id_type=MESH).wait_recv()

    loads = [
        pltpu.make_async_copy(w_hbm, wbuf.at[dp], lsem.at[0]),
        pltpu.make_async_copy(enc_hbm, encbuf.at[sq], lsem.at[1]),
        pltpu.make_async_copy(q_hbm, qg.at[0], lsem.at[2]),
        pltpu.make_async_copy(g_hbm, qg.at[1], lsem.at[3]),
    ]
    for cp in loads:
        cp.start()
    barrier = pltpu.get_barrier_semaphore()
    for dev in (right_y, left_y, right2_y, left2_y, outer, far, out_pair, in_pair, inner, right_x, left_x, sib):
        pl.semaphore_signal(barrier, inc=1, device_id=dev, device_id_type=MESH)
    lane = lax.broadcasted_iota(jnp.int32, (8, 128), 1)
    ids_vec = jnp.zeros((8, 128), jnp.int32)
    for i in range(4):
        ids_vec = jnp.where(lane == i, ids_s[0, i // 2, i % 2], ids_vec)
    ids_v[...] = ids_vec
    pl.semaphore_wait(barrier, 12)

    def shard(dy, kk):
        return ((y + dy + 8) % 8) * 4 + (kk + 8) % 4

    def seq_of(dx, zz):
        return ((x + dx + 4) % 4) * 4 + zz * 2 + c

    def enc_start():
        mine = encbuf.at[sq]
        send(2, ("ez",), enc_hbm, mine, inner)
        send(2, ("ea", "r"), enc_hbm, mine, right_x)
        send(2, ("ea", "l"), enc_hbm, mine, left_x)
        send(2, ("es", 0), enc_hbm, mine, sib)
        send(2, ("ids",), ids_v, sibids_v, sib)

    def enc_z():
        ref = encbuf.at[seq_of(0, 1 - zl)]
        recv(("ez",), ref, inner)
        send(2, ("eb", "r"), ref, ref, right_x)
        send(2, ("eb", "l"), ref, ref, left_x)
        send(2, ("es", 1), ref, ref, sib)

    def enc_1():
        ref = encbuf.at[seq_of(-1, zl)]
        recv(("ea", "r"), ref, left_x)
        send(2, ("e2", "r"), ref, ref, right_x)
        send(2, ("es", 2), ref, ref, sib)
        ref = encbuf.at[seq_of(1, zl)]
        recv(("ea", "l"), ref, right_x)
        send(2, ("es", 3), ref, ref, sib)

    def enc_2():
        ref = encbuf.at[seq_of(1, 1 - zl)]
        recv(("eb", "l"), ref, right_x)
        send(2, ("e2", "l"), ref, ref, left_x)
        send(2, ("es", 4), ref, ref, sib)
        ref = encbuf.at[seq_of(-1, 1 - zl)]
        recv(("eb", "r"), ref, left_x)
        send(2, ("es", 5), ref, ref, sib)

    def enc_3():
        ref = encbuf.at[seq_of(2, zl)]
        recv(("e2", "r"), ref, left_x)
        send(2, ("es", 6), ref, ref, sib)
        ref = encbuf.at[seq_of(2, 1 - zl)]
        recv(("e2", "l"), ref, right_x)
        send(2, ("es", 7), ref, ref, sib)

    def enc_sib():
        cs = 1 - c
        for i, (dx, zz) in enumerate(((0, zl), (0, 1 - zl), (-1, zl), (1, zl), (1, 1 - zl), (-1, 1 - zl), (2, zl), (2, 1 - zl))):
            recv(("es", i), encbuf.at[((x + dx + 4) % 4) * 4 + zz * 2 + cs], sib)

    R0 = (0, CUT)
    RN = (CUT, DE - CUT)

    def part(core, half=None):
        n = RN[core]
        if half is None:
            return R0[core], n
        return pl.multiple_of(R0[core] + half * (n // 2), 16), n // 2

    def wp(d, core, half=None):
        r0, n = part(core, half)
        return wbuf.at[d, pl.ds(r0, n)]

    def own(core, half=None):
        r0, n = part(core, half)
        return w_hbm.at[pl.ds(r0, n)]

    KK = (lambda: k, lambda: k + o, lambda: k - o, lambda: k + 2)

    def to_sib(core, dy, m):
        ref = wp(shard(dy, KK[m]()), core)
        send(core, ("ws", core, dy, m), ref, ref, sib)

    OFFS = (0, -1, 1, -2, 2, -3, 3, 4)

    def y0(dy):
        d = shard(dy, k)
        mine, dst = own(0), wp(d, 0)
        if dy == 0:
            send(0, ("y2r",), mine, dst, right2_y)
            send(0, ("y2l",), mine, dst, left2_y)
            send(0, ("y1r",), mine, dst, right_y)
            send(0, ("y1l",), mine, dst, left_y)
        elif dy == -1:
            recv(("y1r",), dst, left_y)
        elif dy == 1:
            recv(("y1l",), dst, right_y)
        elif dy == -2:
            recv(("y2r",), dst, left2_y)
            send(0, ("y3r",), dst, dst, right_y)
            send(0, ("y4r",), wp(d, 0, 0), wp(d, 0, 0), right2_y)
        elif dy == 2:
            recv(("y2l",), dst, right2_y)
            send(0, ("y3l",), dst, dst, left_y)
            send(0, ("y4l",), wp(d, 0, 1), wp(d, 0, 1), left2_y)
        elif dy == -3:
            recv(("y3r",), dst, left_y)
        elif dy == 3:
            recv(("y3l",), dst, right_y)
        else:
            recv(("y4r",), wp(d, 0, 0), left2_y)
            recv(("y4l",), wp(d, 0, 1), right2_y)

    def z0_start(dy):
        d = shard(dy, k)
        src = own(0) if dy == 0 else wp(d, 0)
        half = own(0, zl) if dy == 0 else wp(d, 0, zl)
        send(0, ("zo", dy), src, wp(d, 0), outer)
        send(0, ("zf", dy), half, wp(d, 0, zl), far)

    def z0_pass(dy):
        ref = wp(shard(dy, k + o), 0)
        recv(("zo", dy), ref, outer)
        send(0, ("zi", dy), ref, ref, inner)
        to_sib(0, dy, 1)
        ref = wp(shard(dy, k + 2), 0, 1 - zl)
        recv(("zf", dy), ref, far)
        send(0, ("zh", dy), ref, ref, inner)

    def z0_last(dy):
        recv(("zi", dy), wp(shard(dy, k - o), 0), inner)
        to_sib(0, dy, 2)
        recv(("zh", dy), wp(shard(dy, k + 2), 0, zl), inner)
        to_sib(0, dy, 3)

    def core0(n):
        if n < 8:
            dy = OFFS[n]
            y0(dy)
            z0_start(dy)
            if n:
                to_sib(0, dy, 0)
        if 3 <= n <= 10:
            z0_pass(OFFS[n - 3])
        if 5 <= n <= 12:
            z0_last(OFFS[n - 5])

    def y1_start(m):
        d = shard(0, KK[m]())
        src = own(1) if m == 0 else wp(d, 1)
        send(1, ("yr", 1, m), src, wp(d, 1), right_y)
        send(1, ("yl", 1, m), src, wp(d, 1), left_y)

    def y1_pass(dy, m):
        d = shard(dy, KK[m]())
        if dy == 4:
            recv(("yr", 4, m), wp(d, 1, 0), left_y)
            recv(("yl", 4, m), wp(d, 1, 1), right_y)
        else:
            nm, to, frm, half = ("yr", right_y, left_y, 0) if dy < 0 else ("yl", left_y, right_y, 1)
            st = abs(dy)
            recv((nm, st, m), wp(d, 1), frm)
            ref = wp(d, 1) if st < 3 else wp(d, 1, half)
            send(1, (nm, st + 1, m), ref, ref, to)
        to_sib(1, dy, m)

    def both(st, m):
        if st < 4:
            y1_pass(-st, m)
            y1_pass(st, m)
        else:
            y1_pass(4, m)

    def core1(n):
        if n == 0:
            d = shard(0, k)
            send(1, ("wo",), own(1), wp(d, 1), outer)
            send(1, ("wd",), own(1), wp(d, 1), out_pair)
            send(1, ("wf",), own(1), wp(d, 1), far)
            y1_start(0)
        elif n == 2:
            for m, nm, frm in ((1, "wo", outer), (2, "wd", in_pair), (3, "wf", far)):
                recv((nm,), wp(shard(0, KK[m]()), 1), frm)
                y1_start(m)
                to_sib(1, 0, m)
        else:
            for sm in {1: ((1, 0),), 3: ((1, 1), (2, 0)), 4: ((1, 2), (1, 3)), 5: ((2, 1), (3, 0)), 6: ((2, 2), (2, 3)),
                       7: ((3, 1), (4, 0)), 8: ((3, 2), (3, 3)), 9: ((4, 1),), 10: ((4, 2),), 11: ((4, 3),), 12: ()}[n]:
                both(*sm)

    def stage(n):
        @pl.when(c == 0)
        def _():
            core0(n)

        @pl.when(c == 1)
        def _():
            core1(n)

    def from_sib(dys):
        for core in range(2):
            @pl.when(c == core)
            def _():
                for dy in dys:
                    for m in range(4):
                        if dy or m:
                            recv(("ws", 1 - core, dy, m), wp(shard(dy, KK[m]()), 1 - core), sib)

    def project(dy):
        base = ((y + dy + 8) % 8) * 4

        def one(i, _):
            d = base + i
            t = d // HEADS
            h = d % HEADS
            lhs = qg[t, :, pl.ds(pl.multiple_of(h * HS, HS), HS)]
            qgw[d] = nt(lhs, wbuf[d]).astype(BF)
            return 0

        lax.fori_loop(0, 4, one, 0, unroll=True)

    def attend(dy, first):
        g = (y + dy + 8) % 4

        def one(s, _):
            rows = pl.ds(pl.multiple_of(s * SPAN, SPAN), SPAN)
            xs = xrd[s]
            qw = qgw[pl.ds(g * 4, 4), rows, :].reshape(4 * SPAN, DE)
            gw = qgw[pl.ds(HEADS + g * 4, 4), rows, :].reshape(4 * SPAN, DE)
            e = jnp.exp(nt(qw, xs) * SCALE)
            probs = e / jnp.sum(e, axis=-1, keepdims=True)
            d_probs = nt(gw, xs)
            delta = jnp.sum(probs * d_probs, axis=-1, keepdims=True)
            ds = (probs * (d_probs - delta) * SCALE).astype(BF)
            pb = probs.astype(BF)
            pbuf[s, pl.ds(g * 4, 4)] = pb.reshape(4, SPAN, HS)
            dsbuf[s, pl.ds(g * 4, 4)] = ds.reshape(4, SPAN, HS)
            new = tn(ds, qw) + tn(pb, gw)
            if first:
                acc[s] = new
            else:
                acc[s] = acc[s] + new
            return 0

        lax.fori_loop(0, 2, one, 0, unroll=True)

    def outputs(dy):
        g = (y + dy + 8) % 4
        for t, buf, out in ((0, dsbuf, dqv), (1, pbuf, attv)):
            for s in range(2):
                lhs = buf[s, pl.ds(g * 4, 4)].reshape(4 * SPAN, HS)
                px[t, :, s] = nn(lhs, xrd[s]).astype(BF).reshape(4, SPAN, DE)
            for i in range(4):
                h = g * 4 + i
                res = nn(px[t, i].reshape(2 * SPAN, DE), wbuf[t * HEADS + h])
                out[:, pl.ds(pl.multiple_of(h * HS, HS), HS)] = res.astype(BF)

    enc_start()
    stage(0)
    stage(1)
    stage(2)
    enc_z()
    stage(3)
    enc_1()
    for cp in loads:
        cp.wait()
    stage(4)
    stage(5)
    from_sib((0,))
    project(0)
    stage(6)
    enc_2()
    stage(7)
    from_sib((-1, 1))
    project(-1)
    project(1)
    stage(8)
    enc_3()
    stage(9)
    from_sib((-2, 2))
    project(-2)
    project(2)
    enc_sib()
    pos = [slot_s[0, ids_s[0, s, r]] for s in range(2) for r in range(2)]
    for s in range(2):
        for r in range(2):
            p = pos[2 * s + r]
            xrd[s, r * NLEN:(r + 1) * NLEN] = encbuf[p // 2, p % 2]
    stage(10)
    recv(("ids",), sibids_v, sib)
    cp = pltpu.make_async_copy(sibids_v, sibids_s, lsem.at[4])
    cp.start()
    attend(2, True)
    from_sib((-3,))
    project(-3)
    attend(1, False)
    cp.wait()
    stage(11)
    from_sib((3,))
    project(3)
    attend(-1, False)
    stage(12)
    from_sib((4,))
    project(4)
    attend(0, False)

    for s in range(2):
        own16[s, 0:2] = acc[s].astype(BF).reshape(2, NLEN, DE)
        own16[s, 2] = jnp.zeros((NLEN, DE), BF)
        sib16[s, 2] = jnp.zeros((NLEN, DE), BF)
    send(2, ("rs",), own16.at[:, 0:2], sib16.at[:, 0:2], sib)
    spos = [slot_s[0, sibids_s[0, s * 2 + r]] for s in range(2) for r in range(2)]

    def which(ps, s, p):
        return jnp.where(ps[2 * s] == p, 0, jnp.where(ps[2 * s + 1] == p, 1, 2))

    def chip_sum(dx, zz, j, rows):
        p = ((x + dx + 4) % 4) * 8 + zz * 4 + 2 * c + j
        total = own16[0, which(pos, 0, p), rows].astype(F32) + own16[1, which(pos, 1, p), rows].astype(F32)
        return total + (sib16[0, which(spos, 0, p), rows].astype(F32) + sib16[1, which(spos, 1, p), rows].astype(F32))

    NA = NLEN // 2
    TOP, BOT, ROWB = slice(0, NA // 2), slice(NA // 2, NA), slice(NA, NLEN)
    DIRS = (("r", right_x, left_x, 1, TOP, BOT), ("l", left_x, right_x, -1, BOT, TOP))

    def far(half):
        for di, (nm, to, _, sg, mine, _) in enumerate(DIRS):
            zz = 1 - zl if half == 0 else zl
            for j in range(2):
                xsend[di, half, j] = chip_sum(2, zz, j, mine).astype(BF)
            send(2, ("x", half, nm), xsend.at[di, half], xrecv.at[di, half], to)

    def near(half):
        for di, (nm, to, _, sg, _, other) in enumerate(DIRS):
            m = 2 if half == 0 else 4
            zz = 1 - zl if half == 0 else zl
            for j in range(2):
                xsend[di, m, j] = chip_sum(sg, zz, j, other).astype(BF)
            send(2, ("x", m, nm), xsend.at[di, m], xrecv.at[di, m], to)

    def near_add(half):
        for di, (nm, to, frm, sg, mine, _) in enumerate(DIRS):
            m = 3 if half == 0 else 5
            zz = 1 - zl if half == 0 else zl
            recv(("x", half, nm), xrecv.at[di, half], frm)
            for j in range(2):
                xsend[di, m, j] = (chip_sum(sg, zz, j, mine) + xrecv[di, half, j].astype(F32)).astype(BF)
            send(2, ("x", m, nm), xsend.at[di, m], xrecv.at[di, m], to)

    def total(half):
        a, b = (2, 3) if half == 0 else (4, 5)
        for di, (nm, _, frm, _, _, _) in enumerate(DIRS):
            for m in (a, b):
                recv(("x", m, nm), xrecv.at[di, m], frm)
        zz = 1 - zl if half == 0 else zl
        for j in range(2):
            top = chip_sum(0, zz, j, TOP) + xrecv[0, b, j].astype(F32) + xrecv[1, a, j].astype(F32)
            bot = chip_sum(0, zz, j, BOT) + xrecv[0, a, j].astype(F32) + xrecv[1, b, j].astype(F32)
            if half == 0:
                zsend[j, TOP] = top.astype(BF)
                zsend[j, BOT] = bot.astype(BF)
            else:
                gout[j, TOP] = top
                gout[j, BOT] = bot

    COLS = (2, 1, -1, 0)

    def b_z(i):
        for j in range(2):
            bzs[i, j] = chip_sum(COLS[i], 1 - zl, j, ROWB).astype(BF)
        send(2, ("bz", i), bzs.at[i], bzr.at[i], inner)

    def b_sum(i, j):
        return chip_sum(COLS[i], zl, j, ROWB) + bzr[i, j].astype(F32)

    def b_far():
        recv(("bz", 0), bzr.at[0], inner)
        for di, (nm, to, _, _, _, _) in enumerate(DIRS):
            bfs[di] = b_sum(0, di).astype(BF)
            send(2, ("bf", nm), bfs.at[di], bfr.at[di], to)

    def b_near():
        for di, (nm, to, _, _, _, _) in enumerate(DIRS):
            recv(("bz", 1 + di), bzr.at[1 + di], inner)
            bns[di, 1 - di] = b_sum(1 + di, 1 - di).astype(BF)
            send(2, ("bn", nm, 0), bns.at[di, 1 - di], bnr.at[di, 1 - di], to)

    def b_near_add():
        for di, (nm, to, frm, _, _, _) in enumerate(DIRS):
            recv(("bf", nm), bfr.at[di], frm)
            bns[di, di] = (b_sum(1 + di, di) + bfr[di].astype(F32)).astype(BF)
            send(2, ("bn", nm, 1), bns.at[di, di], bnr.at[di, di], to)

    def b_total():
        recv(("bz", 3), bzr.at[3], inner)
        for di, (nm, _, frm, _, _, _) in enumerate(DIRS):
            recv(("bn", nm, 0), bnr.at[di, 1 - di], frm)
            recv(("bn", nm, 1), bnr.at[di, di], frm)
        for j in range(2):
            gout[j, ROWB] = b_sum(3, j) + bnr[0, j].astype(F32) + bnr[1, j].astype(F32)

    outputs(1)
    recv(("rs",), sib16.at[:, 0:2], sib)
    far(0)
    b_z(0)
    far(1)
    b_z(1)
    b_z(2)
    near(0)
    b_z(3)
    outputs(-1)
    outputs(2)
    near_add(0)
    near(1)
    b_far()
    near_add(1)
    b_near()
    b_near_add()
    total(0)
    send(2, ("rz",), zsend, zrecv, inner)
    outputs(0)
    total(1)
    b_total()
    recv(("rz",), zrecv, inner)
    for j in range(2):
        gout[j, 0:NA] = gout[j, 0:NA] + zrecv[j].astype(F32)

    def drain(items):
        for i, src, dev in items:
            pltpu.make_async_remote_copy(src, src, ssem.at[i], rsem.at[i], device_id=dev, device_id_type=MESH).wait_send()

    drain(sent[2])
    rows_sent = [[(i, src.shape[0], dev) for i, src, dev in sent[core]] for core in range(2)]

    for core in range(2):
        @pl.when(c == core)
        def _():
            drain([(i, wbuf.at[0, pl.ds(0, n)], dev) for i, n, dev in rows_sent[core]])

    assert len(sem.at) <= NSEM, len(sem.at)


def per_device(queries, grad_out, encoded, kv_weight, neighbour_ids, slot_map):
    anyspec = pl.BlockSpec(memory_space=pltpu.HBM)
    smem = pl.BlockSpec(memory_space=pltpu.SMEM)
    vmem = pl.BlockSpec(memory_space=pltpu.VMEM)
    att, dq, ge = pl.pallas_call(
        kernel,
        out_shape=(
            pltpu.VMEM((2 * SPAN, HEADS * HS), BF),
            pltpu.VMEM((2 * SPAN, HEADS * HS), BF),
            pltpu.VMEM((2, NLEN, DE), F32),
        ),
        in_specs=[anyspec, anyspec, anyspec, anyspec, smem, smem],
        out_specs=(vmem, vmem, vmem),
        scratch_shapes=[
            pltpu.VMEM((NSH, DE, HS), BF),
            pltpu.VMEM((NSEQ, 2, NLEN, DE), BF),
            pltpu.VMEM((2, 2 * SPAN, HEADS * HS), BF),
            pltpu.VMEM((NSH, 2 * SPAN, DE), BF),
            pltpu.VMEM((2, 2 * NLEN, DE), BF),
            pltpu.VMEM((2, HEADS, SPAN, HS), BF),
            pltpu.VMEM((2, HEADS, SPAN, HS), BF),
            pltpu.VMEM((2, 2 * NLEN, DE), F32),
            pltpu.VMEM((2, 3, NLEN, DE), BF),
            pltpu.VMEM((2, 3, NLEN, DE), BF),
            pltpu.VMEM((2, 6, 2, NLEN // 4, DE), BF),
            pltpu.VMEM((2, 6, 2, NLEN // 4, DE), BF),
            pltpu.VMEM((2, NLEN // 2, DE), BF),
            pltpu.VMEM((2, NLEN // 2, DE), BF),
            pltpu.VMEM((4, 2, NLEN // 2, DE), BF),
            pltpu.VMEM((4, 2, NLEN // 2, DE), BF),
            pltpu.VMEM((2, NLEN // 2, DE), BF),
            pltpu.VMEM((2, NLEN // 2, DE), BF),
            pltpu.VMEM((2, 2, NLEN // 2, DE), BF),
            pltpu.VMEM((2, 2, NLEN // 2, DE), BF),
            pltpu.VMEM((2, 4, 2, SPAN, DE), BF),
            pltpu.VMEM((8, 128), jnp.int32),
            pltpu.VMEM((8, 128), jnp.int32),
            pltpu.SMEM((8, 128), jnp.int32),
            pltpu.SemaphoreType.DMA((NSEM,)),
            pltpu.SemaphoreType.DMA((NSEM,)),
            pltpu.SemaphoreType.DMA((8,)),
        ],
        compiler_params=pltpu.CompilerParams(
            collective_id=0, has_side_effects=True, vmem_limit_bytes=58 * 1024 * 1024
        ),
    )(queries[0], grad_out[0], encoded[0], kv_weight, neighbour_ids, slot_map)
    return att[None], dq[None], ge[None]


def solution(mesh):
    in_specs = (
        P("dp", "seq", None),
        P("dp", "seq", None),
        P("dp", "seq", None, None),
        P(None, "dp"),
        P("dp", "seq", None),
        P("dp", None),
    )
    out_specs = (P("dp", "seq", None), P("dp", "seq", None), P("dp", "seq", None, None))
    return jax.shard_map(
        per_device, mesh=mesh, in_specs=in_specs, out_specs=out_specs, check_vma=False
    )
```
